128 devices in a mesh: dp: 4 (over z), fsdp: 32 (over x, y, core).
Axes of the slice: x: 4, y: 4, z: 4, core: 2. Of those that a mesh axis runs over, the one named last changes fastest.
Arguments:
- tokens: bfloat16 [32768, 6144], P(('dp', 'fsdp')), may hold values from -6 to 6
- cotangent: bfloat16 [32768, 6144], P(('dp', 'fsdp')), may hold values from -6 to 6
- up_weight_blocks: bfloat16 [128, 128, 128], P('fsdp'), may hold values from -0.5 to 0.5
- down_weight_blocks: bfloat16 [128, 128, 128], P('fsdp'), may hold values from -0.5 to 0.5
- block_rows: int32 [128], replicated, may hold values from 0 to 47, as said below
- block_cols: int32 [128], replicated, may hold values from 0 to 191
- owner_counts: int32 [32], replicated, may hold values from 1 to 4, as said below
Outputs:
- output: bfloat16 [32768, 6144], P(('dp', 'fsdp'))
- input_grad: bfloat16 [32768, 6144], P(('dp', 'fsdp'))
- up_grad: float32 [128, 128, 128], P('fsdp')
- down_grad: float32 [128, 128, 128], P('fsdp')
The draws below stay inside these ranges and needn't reach their ends.
Inputs may be any that keep to these rules, and one draw needn't show every extreme that they name: Owner o has owner_counts[o] live slots, its first ones; some owner has all 4 live. All 128 slots name distinct (block_rows, block_cols) pairs.
All inputs are finite; a program needn't handle non-finite values.
Results may differ from the reference program's by a relative error of at most 0.0049.
Values may be sent and summed in bfloat16 or wider, within the bound.
A program may use at most 256 MiB of HBM per device.

```python
import math
import jax
import jax.numpy as jnp
from jax import lax

D = 6144
BLOCK_EDGE = 128
SLOTS = 4
TOK_DEV = 256
ROWB = 48
COLB = 192
SLOT_TOTAL = 128
TOKENS = 32768
N_FSDP = 32


def pick_cells(key):
    base_key = jax.random.fold_in(key, 11)
    leading_key, second_key = jax.random.split(base_key)
    lattice_cells = ROWB * COLB
    slot_ordering = jax.random.permutation(leading_key, lattice_cells - 2)[:SLOT_TOTAL] + 1
    owner_pair = jax.random.permutation(second_key, N_FSDP)[:2] * SLOTS
    cells = slot_ordering.at[owner_pair[0]].set(lattice_cells - 1)
    cells = cells.at[owner_pair[1]].set(0)
    return cells.astype(jnp.int32)


def draw_block_rows(key, part):
    return (pick_cells(key) // COLB).astype(jnp.int32)


def draw_block_cols(key, part):
    return (pick_cells(key) % COLB).astype(jnp.int32)


def draw_owner_counts(key, part):
    base_key = jax.random.fold_in(key, 23)
    leading_key, second_key = jax.random.split(base_key)
    base_counts = jax.random.randint(leading_key, (N_FSDP,), 1, SLOTS // 2 + 1)
    full_owners = jax.random.permutation(second_key, N_FSDP)[:max(1, N_FSDP // 8)]
    return base_counts.at[full_owners].set(SLOTS).astype(jnp.int32)


def block_scale(key, dims, shards, smallest, largest):
    factor_of, own = 1.0, jax.random.fold_in(key, 6)
    for position, shards_of in shards:
        heights = jnp.exp(jax.random.uniform(jax.random.fold_in(own, position), (shards_of,), jnp.float32, smallest / len(shards), largest / len(shards)))
        factor_of = factor_of * jnp.repeat(heights, dims[position] // shards_of).reshape([-1 if axis == position else 1 for axis in range(len(dims))])
    return factor_of


def gaussian(key, dims, deviation, bound, shards=(), kind=jnp.bfloat16):
    drawn = jax.random.normal(key, dims, jnp.float32) * deviation
    if len(shards) > 0:
        drawn = block_scale(key, dims, shards, -0.22, 0.18) * drawn
    return jnp.clip(drawn, min=-bound, max=bound).astype(kind)


def setup_inputs(seed: int = 0) -> dict:
    seeds = jax.random.split(jax.random.key(seed), 8)
    return {
        "tokens": gaussian(seeds[0], (TOKENS, D), 1.0, 6.0, ((0, 128),)),
        "cotangent": gaussian(seeds[1], (TOKENS, D), 1.0, 6.0, ((0, 128),)),
        "up_weight_blocks": gaussian(seeds[2], (SLOT_TOTAL, BLOCK_EDGE, BLOCK_EDGE), BLOCK_EDGE ** -0.5, 0.5, ((0, 32),)),
        "down_weight_blocks": gaussian(seeds[3], (SLOT_TOTAL, BLOCK_EDGE, BLOCK_EDGE), BLOCK_EDGE ** -0.5, 0.5, ((0, 32),)),
        "block_rows": draw_block_rows(jax.random.fold_in(seeds[7], 71), 0),
        "block_cols": draw_block_cols(jax.random.fold_in(seeds[7], 71), 0),
        "owner_counts": draw_owner_counts(jax.random.fold_in(seeds[7], 71), 0),
    }


gelu_scale = 0.7978845608028654
cubic_coef = 0.044715

def gelu_parts(values):
    inner_arg = gelu_scale * (values + cubic_coef * values * values * values)
    tanh_val = jnp.tanh(inner_arg)
    gelu_value = 0.5 * values * (1.0 + tanh_val)
    gelu_slope = 0.5 * (1.0 + tanh_val) + 0.5 * values * (1.0 - tanh_val * tanh_val) * gelu_scale * (1.0 + 3.0 * cubic_coef * values * values)
    return (gelu_value, gelu_slope)

def rounded(source):
    return lax.optimization_barrier(source.astype(jnp.bfloat16)).astype(jnp.float32)

def reference(tokens, cotangent, up_weight_blocks, down_weight_blocks, block_rows, block_cols, owner_counts):
    slot_position = jnp.arange(SLOT_TOTAL, dtype=jnp.int32)
    live_mask = slot_position % SLOTS < owner_counts[slot_position // SLOTS]
    mask_f = live_mask.astype(jnp.float32)[:, None, None]
    up_f = up_weight_blocks.astype(jnp.float32) * mask_f
    down_f = down_weight_blocks.astype(jnp.float32) * mask_f
    group_total = TOKENS // TOK_DEV

    def to_blocks(source):
        return source.reshape(TOK_DEV, source.shape[1] // BLOCK_EDGE, BLOCK_EDGE).transpose(1, 0, 2)

    def from_blocks(blocks):
        return blocks.transpose(1, 0, 2).reshape(TOK_DEV, blocks.shape[0] * BLOCK_EDGE)

    def one_group(state_pair, group_number):
        first_row = (group_number * TOK_DEV).astype(jnp.int32)
        x_blocks = to_blocks(lax.dynamic_slice_in_dim(tokens, first_row, TOK_DEV, 0).astype(jnp.float32))
        dy_blocks = to_blocks(lax.dynamic_slice_in_dim(cotangent, first_row, TOK_DEV, 0).astype(jnp.float32))
        x_pick = x_blocks[block_rows]
        pre_act = jax.ops.segment_sum(jnp.einsum('snk,skj->snj', x_pick, up_f), block_cols, num_segments=COLB)
        gelu_value, gelu_slope = gelu_parts(pre_act)
        hidden = rounded(gelu_value)
        h_pick = hidden[block_cols]
        out_blocks = jax.ops.segment_sum(jnp.einsum('snk,skj->snj', h_pick, down_f), block_rows, num_segments=ROWB)
        dy_pick = dy_blocks[block_rows]
        hidden_grad = jax.ops.segment_sum(jnp.einsum('snj,skj->snk', dy_pick, down_f), block_cols, num_segments=COLB)
        pre_grad = rounded(hidden_grad * gelu_slope)
        p_pick = pre_grad[block_cols]
        in_blocks = jax.ops.segment_sum(jnp.einsum('snj,skj->snk', p_pick, up_f), block_rows, num_segments=ROWB)
        up_part = jnp.einsum('snk,snj->skj', x_pick, p_pick) * mask_f
        down_part = jnp.einsum('snk,snj->skj', h_pick, dy_pick) * mask_f
        next_pair = (state_pair[0] + up_part, state_pair[1] + down_part)
        outs_pair = (from_blocks(out_blocks).astype(jnp.bfloat16), from_blocks(in_blocks).astype(jnp.bfloat16))
        return (next_pair, outs_pair)
    empty_gradients = (jnp.zeros((SLOT_TOTAL, BLOCK_EDGE, BLOCK_EDGE), jnp.float32), jnp.zeros((SLOT_TOTAL, BLOCK_EDGE, BLOCK_EDGE), jnp.float32))
    sums_pair, stacked = lax.scan(one_group, empty_gradients, jnp.arange(group_total, dtype=jnp.int32))
    grad_scale = 1.0 / math.sqrt(TOKENS)
    output = stacked[0].reshape(TOKENS, D)
    input_grad = stacked[1].reshape(TOKENS, D)
    return (output, input_grad, sums_pair[0] * grad_scale, sums_pair[1] * grad_scale)
```

```python
import functools
import math

import jax
import jax.numpy as jnp
from jax import lax
from jax.experimental import pallas as pl
from jax.experimental.pallas import tpu as pltpu
from jax.sharding import PartitionSpec as P

EDGE = 128
SLOTS = 4
RING = 4
MESH_ID = pl.DeviceIdType.MESH
BF16 = jnp.bfloat16
F32 = jnp.float32

gelu_scale = 0.7978845608028654
cubic_coef = 0.044715


def gelu_parts(values):
    inner_arg = gelu_scale * (values + cubic_coef * values * values * values)
    tanh_val = jnp.tanh(inner_arg)
    gelu_value = 0.5 * values * (1.0 + tanh_val)
    gelu_slope = 0.5 * (1.0 + tanh_val) + 0.5 * values * (
        1.0 - tanh_val * tanh_val
    ) * gelu_scale * (1.0 + 3.0 * cubic_coef * values * values)
    return gelu_value, gelu_slope


class Spot:
    def __init__(self):
        me = lax.axis_index("fsdp")
        self.z = lax.axis_index("dp")
        self.c = lax.rem(me, 2)
        self.y = lax.rem(me // 2, RING)
        self.x = me // (2 * RING)

    def owner(self, i, j, c=None):
        c = self.c if c is None else c
        x = lax.rem(self.x + i * (1 - c) + j * c, RING)
        y = lax.rem(self.y + i * c + j * (1 - c), RING)
        return (x * RING + y) * 2 + c

    def sibling(self):
        return (self.x * RING + self.y) * 2 + (1 - self.c)


def greet(targets):
    barrier = pltpu.get_barrier_semaphore()
    for target in targets:
        pl.semaphore_signal(barrier, inc=1, device_id=target, device_id_type=MESH_ID)
    pl.semaphore_wait(barrier, len(targets))


class Mail:
    def __init__(self, send_sem, recv_sem):
        self.send_sem, self.recv_sem = send_sem, recv_sem
        self.keys, self.sent = {}, []

    def slot(self, key):
        return self.keys.setdefault(key, len(self.keys))

    def send(self, src, dst, target, key):
        copy = pltpu.make_async_remote_copy(
            src_ref=src,
            dst_ref=dst,
            send_sem=self.send_sem.at[len(self.sent)],
            recv_sem=self.recv_sem.at[self.slot(key)],
            device_id=target,
            device_id_type=MESH_ID,
        )
        copy.start()
        self.sent.append(copy)

    def wait(self, dst, key, target):
        pltpu.make_async_remote_copy(
            src_ref=dst,
            dst_ref=dst,
            send_sem=self.send_sem.at[0],
            recv_sem=self.recv_sem.at[self.slot(key)],
            device_id=target,
            device_id_type=MESH_ID,
        ).wait_recv()

    def finish(self):
        for copy in self.sent:
            copy.wait_send()


AG_COPIES = 62


def gather_kernel(up_ref, dn_ref, gu_ref, gd_ref, own_sem, send_sem, recv_sem):
    spot = Spot()
    mine = (up_ref, dn_ref)
    full = (gu_ref, gd_ref)
    first_p, first_m = {"fsdp": spot.owner(1, 0)}, {"fsdp": spot.owner(3, 0)}
    second_p, second_m = {"fsdp": spot.owner(0, 1)}, {"fsdp": spot.owner(0, 3)}
    other = {"fsdp": spot.sibling()}
    greet([first_p, first_m, second_p, second_m, other])
    mail = Mail(send_sem, recv_sem)
    me = spot.owner(0, 0)

    def held(i, j, h):
        return mine[h] if (i, j) == (0, 0) else full[h].at[spot.owner(i, j)]

    def place(i, j, h):
        return full[h].at[spot.owner(i, j)]

    def arrive(i, j, h, key, source):
        mail.wait(place(i, j, h), key, source)

    def share(i, j, h):
        mail.send(held(i, j, h), place(i, j, h), other, ("sib", i, j, h))

    def second(i, h):
        mail.send(held(i, 0, h), place(i, 0, h), second_p, ("sec", i, 3, h))
        mail.send(held(i, 0, h), place(i, 0, h), second_m, ("sec", i, 1, h))

    keeps = [pltpu.make_async_copy(mine[h], full[h].at[me], own_sem.at[h]) for h in (0, 1)]
    for h in (0, 1):
        mail.send(mine[h], place(0, 0, h), first_p, ("fst", 3, h))
        mail.send(mine[1 - h], place(0, 0, 1 - h), first_m, ("fst", 1, 1 - h))
    for h in (0, 1):
        second(0, h)
    for h in (0, 1):
        share(0, 0, h)
        keeps[h].start()
    arrive(3, 0, 0, ("fst", 3, 0), first_m)
    mail.send(held(3, 0, 0), place(3, 0, 0), first_p, ("fst", 2, 0))
    arrive(1, 0, 1, ("fst", 1, 1), first_p)
    mail.send(held(1, 0, 1), place(1, 0, 1), first_m, ("fst", 2, 1))
    second(3, 0)
    second(1, 1)
    share(3, 0, 0)
    share(1, 0, 1)
    arrive(3, 0, 1, ("fst", 3, 1), first_m)
    second(3, 1)
    share(3, 0, 1)
    arrive(1, 0, 0, ("fst", 1, 0), first_p)
    second(1, 0)
    share(1, 0, 0)
    arrive(2, 0, 0, ("fst", 2, 0), first_m)
    second(2, 0)
    share(2, 0, 0)
    arrive(2, 0, 1, ("fst", 2, 1), first_p)
    second(2, 1)
    share(2, 0, 1)
    for i in (0, 3, 1, 2):
        arrive(i, 3, 0, ("sec", i, 3, 0), second_m)
        mail.send(held(i, 3, 0), place(i, 3, 0), second_p, ("sec", i, 2, 0))
        share(i, 3, 0)
        arrive(i, 1, 1, ("sec", i, 1, 1), second_p)
        mail.send(held(i, 1, 1), place(i, 1, 1), second_m, ("sec", i, 2, 1))
        share(i, 1, 1)
        arrive(i, 3, 1, ("sec", i, 3, 1), second_m)
        share(i, 3, 1)
        arrive(i, 1, 0, ("sec", i, 1, 0), second_p)
        share(i, 1, 0)
    for i in (0, 3, 1, 2):
        arrive(i, 2, 0, ("sec", i, 2, 0), second_m)
        share(i, 2, 0)
        arrive(i, 2, 1, ("sec", i, 2, 1), second_p)
        share(i, 2, 1)
    for i in range(RING):
        for j in range(RING):
            for h in (0, 1):
                mail.wait(full[h].at[spot.owner(i, j, 1 - spot.c)], ("sib", i, j, h), other)
    for keep in keeps:
        keep.wait()
    mail.finish()
    assert len(mail.sent) == len(mail.keys) == AG_COPIES


def gather_weights(up, dn):
    owners = 2 * RING * RING
    full = jax.ShapeDtypeStruct((owners,) + up.shape, up.dtype)
    return pl.pallas_call(
        gather_kernel,
        out_shape=(full, full),
        in_specs=[pl.BlockSpec(memory_space=pl.ANY)] * 2,
        out_specs=(pl.BlockSpec(memory_space=pl.ANY),) * 2,
        scratch_shapes=[
            pltpu.SemaphoreType.DMA((2,)),
            pltpu.SemaphoreType.DMA((AG_COPIES,)),
            pltpu.SemaphoreType.DMA((AG_COPIES,)),
        ],
        compiler_params=pltpu.CompilerParams(collective_id=0, has_side_effects=True),
        name="gather_weights",
    )(up, dn)


NT = (((1,), (1,)), ((), ()))
TN = (((0,), (0,)), ((), ()))
NN = (((1,), (0,)), ((), ()))


def mm(a, b, dims):
    return lax.dot_general(a, b, dims, preferred_element_type=F32)


UNROLL = 2


def layer_kernel(
    rows, cols, counts,
    x_hbm, dy_hbm, up_hbm, dn_hbm,
    out_hbm, in_hbm, pu_hbm, pd_hbm,
    x, dy, up, dn, out, inp, hid, pgr, pu, pd, acc,
    col_at, row_at, by_col, by_row, sem,
):
    total = rows.shape[0]
    tok, width = x_hbm.shape
    row_blocks = width // EDGE
    col_blocks = col_at.shape[0] - 2
    loads = [
        pltpu.make_async_copy(src, dst, sem.at[n])
        for n, (src, dst) in enumerate(((x_hbm, x), (dy_hbm, dy), (up_hbm, up), (dn_hbm, dn)))
    ]
    for load in loads:
        load.start()

    def clear(ref):
        def step(n, carry):
            ref[n] = 0
            return carry
        lax.fori_loop(0, ref.shape[0], step, 0)

    clear(col_at)
    clear(row_at)

    def live(k):
        return lax.rem(k, SLOTS) < counts[k // SLOTS]

    def count(k, carry):
        @pl.when(live(k))
        def _():
            col_at[cols[k] + 2] = col_at[cols[k] + 2] + 1
            row_at[rows[k] + 2] = row_at[rows[k] + 2] + 1
        return carry

    lax.fori_loop(0, total, count, 0)

    def prefix(ref):
        def step(n, carry):
            ref[n] = ref[n] + ref[n - 1]
            return carry
        lax.fori_loop(1, ref.shape[0], step, 0)

    prefix(col_at)
    prefix(row_at)
    n_live = col_at[col_blocks + 1]

    def order(k, carry):
        @pl.when(live(k))
        def _():
            c, r = cols[k] + 1, rows[k] + 1
            by_col[col_at[c]] = k
            col_at[c] = col_at[c] + 1
            by_row[row_at[r]] = k
            row_at[r] = row_at[r] + 1
        return carry

    lax.fori_loop(0, total, order, 0)
    for u in range(UNROLL):
        by_col[n_live + u] = by_col[n_live - 1]
        by_row[n_live + u] = by_row[n_live - 1]

    def zero_cols(b, carry):
        at = pl.ds(pl.multiple_of(b * EDGE, EDGE), EDGE)
        out[:, at] = jnp.zeros((tok, EDGE), BF16)
        inp[:, at] = jnp.zeros((tok, EDGE), BF16)
        return carry

    lax.fori_loop(0, row_blocks, zero_cols, 0)

    def zero_dead(k, carry):
        @pl.when(jnp.logical_not(live(k)))
        def _():
            pu[k] = jnp.zeros((EDGE, EDGE), BF16)
            pd[k] = jnp.zeros((EDGE, EDGE), BF16)
        return carry

    lax.fori_loop(0, total, zero_dead, 0)
    for load in loads:
        load.wait()

    def block(b):
        return pl.ds(pl.multiple_of(b * EDGE, EDGE), EDGE)

    steps = (n_live + UNROLL - 1) // UNROLL

    def forward(step, carry):
        pre, back = acc[0], acc[1]
        for u in range(UNROLL):
            s = step * UNROLL + u
            k = by_col[s]
            at = block(rows[k])
            first = jnp.logical_or(s == 0, cols[by_col[jnp.maximum(s - 1, 0)]] != cols[k])
            pre = jnp.where(first, 0.0, pre) + mm(x[:, at], up[k], NN)
            back = jnp.where(first, 0.0, back) + mm(dy[:, at], dn[k], NT)
            value, slope = gelu_parts(pre)
            hid[s] = value.astype(BF16)
            pgr[s] = (back * slope).astype(BF16)
        acc[0] = pre
        acc[1] = back
        return carry

    lax.fori_loop(0, steps, forward, 0)

    def backward(step, carry):
        o, g = acc[0], acc[1]
        for u in range(UNROLL):
            t = step * UNROLL + u
            k = by_row[t]
            r = rows[k]
            at = block(r)
            to = block(jnp.where(t < n_live, r, row_blocks))
            first = jnp.logical_or(t == 0, rows[by_row[jnp.maximum(t - 1, 0)]] != r)
            last = col_at[cols[k] + 1] - 1
            h, p = hid[last], pgr[last]
            o = jnp.where(first, 0.0, o) + mm(h, dn[k], NN)
            g = jnp.where(first, 0.0, g) + mm(p, up[k], NT)
            out[:, to] = o.astype(BF16)
            inp[:, to] = g.astype(BF16)
            pu[k] = mm(x[:, at], p, TN).astype(BF16)
            pd[k] = mm(h, dy[:, at], TN).astype(BF16)
        acc[0] = o
        acc[1] = g
        return carry

    lax.fori_loop(0, steps, backward, 0)
    stores = [
        pltpu.make_async_copy(src, dst, sem.at[n])
        for n, (src, dst) in enumerate((
            (out.at[:, pl.ds(0, width)], out_hbm), (inp.at[:, pl.ds(0, width)], in_hbm),
            (pu, pu_hbm), (pd, pd_hbm),
        ))
    ]
    for store in stores:
        store.start()
    for store in stores:
        store.wait()


def local_layer(rows, cols, counts, x, dy, up, dn, col_blocks):
    tok, width = x.shape
    total = rows.shape[0]
    any_spec = pl.BlockSpec(memory_space=pl.ANY)
    smem_spec = pl.BlockSpec(memory_space=pltpu.SMEM)
    part = jax.ShapeDtypeStruct((total, EDGE, EDGE), BF16)
    return pl.pallas_call(
        layer_kernel,
        out_shape=(
            jax.ShapeDtypeStruct((tok, width), BF16),
            jax.ShapeDtypeStruct((tok, width), BF16),
            part,
            part,
        ),
        in_specs=[smem_spec] * 3 + [any_spec] * 4,
        out_specs=(any_spec,) * 4,
        scratch_shapes=[
            pltpu.VMEM((tok, width), BF16),
            pltpu.VMEM((tok, width), BF16),
            pltpu.VMEM((total, EDGE, EDGE), BF16),
            pltpu.VMEM((total, EDGE, EDGE), BF16),
            pltpu.VMEM((tok, width + EDGE), BF16),
            pltpu.VMEM((tok, width + EDGE), BF16),
            pltpu.VMEM((total + UNROLL, tok, EDGE), BF16),
            pltpu.VMEM((total + UNROLL, tok, EDGE), BF16),
            pltpu.VMEM((total, EDGE, EDGE), BF16),
            pltpu.VMEM((total, EDGE, EDGE), BF16),
            pltpu.VMEM((2, tok, EDGE), F32),
            pltpu.SMEM((col_blocks + 2,), jnp.int32),
            pltpu.SMEM((width // EDGE + 2,), jnp.int32),
            pltpu.SMEM((total + UNROLL,), jnp.int32),
            pltpu.SMEM((total + UNROLL,), jnp.int32),
            pltpu.SemaphoreType.DMA((4,)),
        ],
        compiler_params=pltpu.CompilerParams(vmem_limit_bytes=56 << 20),
        name="local_layer",
    )(rows, cols, counts, x, dy, up.reshape(total, EDGE, EDGE), dn.reshape(total, EDGE, EDGE))


RS_COPIES = 66


def scatter_kernel(
    scale, pu_hbm, pd_hbm, ug_ref, dg_ref,
    own, sib, mid, got_m, got_p, r_bf, r_f32, mid2, fin_m, fin_p, zsend, zrecv,
    own_sem, send_sem, recv_sem,
):
    spot = Spot()
    part = (pu_hbm, pd_hbm)
    final = (ug_ref, dg_ref)
    first_p, first_m = {"fsdp": spot.owner(1, 0)}, {"fsdp": spot.owner(3, 0)}
    second_p, second_m = {"fsdp": spot.owner(0, 1)}, {"fsdp": spot.owner(0, 3)}
    other = {"fsdp": spot.sibling()}
    z_a = {"dp": spot.z + 1 - 2 * lax.rem(spot.z, 2)}
    z_b = {"dp": RING - 1 - spot.z}
    greet([first_p, first_m, second_p, second_m, other, z_a, z_b])
    mail = Mail(send_sem, recv_sem)
    order = [(i, j, h) for j in (2, 1, 3, 0) for i in (2, 1, 3, 0) for h in (0, 1)]
    loads = {}
    for n, (i, j, h) in enumerate(order):
        at = i * RING + j
        theirs = spot.owner(i, j, 1 - spot.c)
        mail.send(part[h].at[theirs], sib.at[h, at], other, ("sib", i, j, h))
        loads[i, j, h] = pltpu.make_async_copy(
            part[h].at[spot.owner(i, j)], own.at[h, at], own_sem.at[n]
        )
        loads[i, j, h].start()

    def pair(i, j, h):
        at = i * RING + j
        loads[i, j, h].wait()
        mail.wait(sib.at[h, at], ("sib", i, j, h), other)
        return own[h, at].astype(F32) + sib[h, at].astype(F32)

    def keep(i, j, h, value):
        at = i * RING + j
        own[h, at] = value.astype(BF16)
        return own.at[h, at]

    ring = (2, 1, 3, 0)
    for i in ring:
        mail.send(keep(i, 2, 0, pair(i, 2, 0)), mid.at[i, 0], second_p, ("mid", i, 0))
        mail.send(keep(i, 2, 1, pair(i, 2, 1)), mid.at[i, 1], second_m, ("mid", i, 1))
    for i in ring:
        mail.send(keep(i, 1, 1, pair(i, 1, 1)), got_m.at[i, 1], second_p, ("m", i, 1))
        mail.send(keep(i, 3, 0, pair(i, 3, 0)), got_p.at[i, 0], second_m, ("p", i, 0))
        near = pair(i, 1, 0)
        mail.wait(mid.at[i, 0], ("mid", i, 0), second_m)
        near = near + mid[i, 0].astype(F32)
        mail.send(keep(i, 1, 0, near), got_m.at[i, 0], second_p, ("m", i, 0))
        near = pair(i, 3, 1)
        mail.wait(mid.at[i, 1], ("mid", i, 1), second_p)
        near = near + mid[i, 1].astype(F32)
        mail.send(keep(i, 3, 1, near), got_p.at[i, 1], second_m, ("p", i, 1))

    def ring_sum(i, h):
        value = pair(i, 0, h)
        mail.wait(got_m.at[i, h], ("m", i, h), second_m)
        mail.wait(got_p.at[i, h], ("p", i, h), second_p)
        return value + got_m[i, h].astype(F32) + got_p[i, h].astype(F32)

    for n, (i, h, dst, target, key) in enumerate((
        (2, 0, mid2.at[0], first_p, ("mid2", 0)),
        (2, 1, mid2.at[1], first_m, ("mid2", 1)),
        (1, 1, fin_m.at[1], first_p, ("fm", 1)),
        (3, 0, fin_p.at[0], first_m, ("fp", 0)),
    )):
        r_bf[n] = ring_sum(i, h).astype(BF16)
        mail.send(r_bf.at[n], dst, target, key)
    for n, (i, h, dst, target, key, source) in enumerate((
        (1, 0, fin_m.at[0], first_p, ("fm", 0), first_m),
        (3, 1, fin_p.at[1], first_m, ("fp", 1), first_p),
    )):
        r_f32[n] = ring_sum(i, h)
        mail.wait(mid2.at[h], ("mid2", h), source)
        r_bf[4 + n] = (r_f32[n] + mid2[h].astype(F32)).astype(BF16)
        mail.send(r_bf.at[4 + n], dst, target, key)
    for h in (0, 1):
        r_f32[h] = ring_sum(0, h)
    for h in (0, 1):
        mail.wait(fin_m.at[h], ("fm", h), first_m)
        mail.wait(fin_p.at[h], ("fp", h), first_p)
        value = r_f32[h] + fin_m[h].astype(F32) + fin_p[h].astype(F32)
        zsend[0, h] = value.astype(BF16)
        mail.send(zsend.at[0, h], zrecv.at[0, h], (z_a, z_b)[h], ("z", 0, h))
    for h in (0, 1):
        mail.wait(zrecv.at[0, h], ("z", 0, h), (z_a, z_b)[h])
        value = zsend[0, h].astype(F32) + zrecv[0, h].astype(F32)
        zsend[1, h] = value.astype(BF16)
        mail.send(zsend.at[1, h], zrecv.at[1, h], (z_b, z_a)[h], ("z", 1, h))
    for h in (0, 1):
        mail.wait(zrecv.at[1, h], ("z", 1, h), (z_b, z_a)[h])
        value = zsend[1, h].astype(F32) + zrecv[1, h].astype(F32)
        final[h][...] = value * scale
    mail.finish()
    assert len(mail.sent) == len(mail.keys) == RS_COPIES


def scatter_grads(pu, pd, scale):
    owners = 2 * RING * RING
    piece = (SLOTS, EDGE, EDGE)
    grad = jax.ShapeDtypeStruct(piece, F32)
    vmem = pl.BlockSpec(memory_space=pltpu.VMEM)
    return pl.pallas_call(
        functools.partial(scatter_kernel, scale),
        out_shape=(grad, grad),
        in_specs=[pl.BlockSpec(memory_space=pl.ANY)] * 2,
        out_specs=(vmem, vmem),
        scratch_shapes=[
            pltpu.VMEM((2, RING * RING) + piece, BF16),
            pltpu.VMEM((2, RING * RING) + piece, BF16),
            pltpu.VMEM((RING, 2) + piece, BF16),
            pltpu.VMEM((RING, 2) + piece, BF16),
            pltpu.VMEM((RING, 2) + piece, BF16),
            pltpu.VMEM((6,) + piece, BF16),
            pltpu.VMEM((2,) + piece, F32),
            pltpu.VMEM((2,) + piece, BF16),
            pltpu.VMEM((2,) + piece, BF16),
            pltpu.VMEM((2,) + piece, BF16),
            pltpu.VMEM((2, 2) + piece, BF16),
            pltpu.VMEM((2, 2) + piece, BF16),
            pltpu.SemaphoreType.DMA((2 * RING * RING,)),
            pltpu.SemaphoreType.DMA((RS_COPIES,)),
            pltpu.SemaphoreType.DMA((RS_COPIES,)),
        ],
        compiler_params=pltpu.CompilerParams(
            collective_id=1, has_side_effects=True, vmem_limit_bytes=48 << 20
        ),
        name="scatter_grads",
    )(pu.reshape((owners,) + piece), pd.reshape((owners,) + piece))


COL_BLOCKS = 192


def on_device(tokens, cotangent, up_w, dn_w, block_rows, block_cols, owner_counts):
    devices = lax.axis_size("dp") * lax.axis_size("fsdp")
    scale = 1.0 / math.sqrt(tokens.shape[0] * devices)
    up_full, dn_full = gather_weights(up_w, dn_w)
    output, input_grad, up_part, dn_part = local_layer(
        block_rows, block_cols, owner_counts, tokens, cotangent, up_full, dn_full, COL_BLOCKS
    )
    up_grad, down_grad = scatter_grads(up_part, dn_part, scale)
    return output, input_grad, up_grad, down_grad


def solution(mesh):
    in_specs = (
        P(("dp", "fsdp"), None),
        P(("dp", "fsdp"), None),
        P("fsdp", None, None),
        P("fsdp", None, None),
        P(),
        P(),
        P(),
    )
    out_specs = (
        P(("dp", "fsdp"), None),
        P(("dp", "fsdp"), None),
        P("fsdp", None, None),
        P("fsdp", None, None),
    )
    return jax.shard_map(
        on_device, mesh=mesh, in_specs=in_specs, out_specs=out_specs, check_vma=False
    )
```

```python
import functools
import math

import jax
import jax.numpy as jnp
from jax import lax
from jax.experimental import pallas as pl
from jax.experimental.pallas import tpu as pltpu
from jax.sharding import PartitionSpec as P

EDGE = 128
SLOTS = 4
RING = 4
MESH_ID = pl.DeviceIdType.MESH
BF16 = jnp.bfloat16
F32 = jnp.float32

gelu_scale = 0.7978845608028654
cubic_coef = 0.044715


def gelu_parts(values):
    inner_arg = gelu_scale * (values + cubic_coef * values * values * values)
    tanh_val = jnp.tanh(inner_arg)
    gelu_value = 0.5 * values * (1.0 + tanh_val)
    gelu_slope = 0.5 * (1.0 + tanh_val) + 0.5 * values * (
        1.0 - tanh_val * tanh_val
    ) * gelu_scale * (1.0 + 3.0 * cubic_coef * values * values)
    return gelu_value, gelu_slope


class Spot:
    def __init__(self):
        me = lax.axis_index("fsdp")
        self.z = lax.axis_index("dp")
        self.c = lax.rem(me, 2)
        self.y = lax.rem(me // 2, RING)
        self.x = me // (2 * RING)

    def owner(self, i, j, c=None):
        c = self.c if c is None else c
        x = lax.rem(self.x + i * (1 - c) + j * c, RING)
        y = lax.rem(self.y + i * c + j * (1 - c), RING)
        return (x * RING + y) * 2 + c

    def sibling(self):
        return (self.x * RING + self.y) * 2 + (1 - self.c)


def greet(targets):
    barrier = pltpu.get_barrier_semaphore()
    for target in targets:
        pl.semaphore_signal(barrier, inc=1, device_id=target, device_id_type=MESH_ID)
    pl.semaphore_wait(barrier, len(targets))


class Mail:
    def __init__(self, send_sem, recv_sem):
        self.send_sem, self.recv_sem = send_sem, recv_sem
        self.keys, self.sent = {}, []

    def slot(self, key):
        return self.keys.setdefault(key, len(self.keys))

    def send(self, src, dst, target, key):
        copy = pltpu.make_async_remote_copy(
            src_ref=src,
            dst_ref=dst,
            send_sem=self.send_sem.at[len(self.sent)],
            recv_sem=self.recv_sem.at[self.slot(key)],
            device_id=target,
            device_id_type=MESH_ID,
        )
        copy.start()
        self.sent.append(copy)

    def wait(self, dst, key, target):
        pltpu.make_async_remote_copy(
            src_ref=dst,
            dst_ref=dst,
            send_sem=self.send_sem.at[0],
            recv_sem=self.recv_sem.at[self.slot(key)],
            device_id=target,
            device_id_type=MESH_ID,
        ).wait_recv()

    def finish(self):
        for copy in self.sent:
            copy.wait_send()

    def copy_at(self, src, dst, target, n):
        return pltpu.make_async_remote_copy(
            src_ref=src,
            dst_ref=dst,
            send_sem=self.send_sem.at[n],
            recv_sem=self.recv_sem.at[n],
            device_id=target,
            device_id_type=MESH_ID,
        )

    def send_at(self, src, dst, target, n):
        self.copy_at(src, dst, target, n).start()

    def wait_at(self, dst, target, n):
        self.copy_at(dst, dst, target, n).wait_recv()

    def sent_at(self, src, target, n):
        self.copy_at(src, src, target, n).wait_send()


VM_K1 = 8 << 20
AG_COPIES = 62
SLOT_TOTAL = 128
DEAD = SLOT_TOTAL
BY_COL, BY_ROW, LAST, LIVE = 0, 1, 2, 3


def slot_tables(rows_ref, cols_ref, counts, tab_ref):
    n = SLOT_TOTAL
    lane = lax.broadcasted_iota(jnp.int32, (n, n), 1)
    sub = lax.broadcasted_iota(jnp.int32, (n, n), 0)
    lane_owner = lax.broadcasted_iota(jnp.int32, (8, n), 1) // SLOTS
    held = jnp.zeros((8, n), jnp.int32)
    for o in range(n // SLOTS):
        held = jnp.where(lane_owner == o, counts[o], held)
    lane_f, sub_f = lane.astype(F32), sub.astype(F32)

    def spread(row):
        across = jnp.broadcast_to(row.astype(F32), (n, n))
        return across, across.T

    held_l, held_s = spread(held[0:1])
    slot_l = lax.rem(lane, SLOTS).astype(F32)
    slot_s = lax.rem(sub, SLOTS).astype(F32)
    live_l = jnp.where(slot_l < held_l, 1.0, 0.0)
    live_s = jnp.where(slot_s < held_s, 1.0, 0.0)

    def order(key_l, key_s):
        tie = jnp.where(key_l == key_s, jnp.where(lane < sub, live_l, 0.0), 0.0)
        rank = jnp.sum(jnp.where(key_l < key_s, live_l, tie), axis=1, keepdims=True)
        hit = jnp.where(rank == lane_f, live_s, 0.0)
        return jnp.sum(hit * sub_f, axis=0, keepdims=True)

    col_l, col_s = spread(cols_ref[...])
    row_l, row_s = spread(rows_ref[...])
    upto = jnp.sum(jnp.where(col_s <= col_l, live_s, 0.0), axis=0, keepdims=True)
    last = jnp.where(live_l[0:1] > 0.5, upto - 1.0, float(DEAD))
    number = jnp.sum(live_s, axis=0, keepdims=True)
    for at, row in (
        (BY_COL, order(col_l, col_s)), (BY_ROW, order(row_l, row_s)), (LAST, last), (LIVE, number)
    ):
        tab_ref[at:at + 1, :] = row.astype(jnp.int32)


def gather_kernel(
    rows_ref, cols_ref, counts, up_ref, dn_ref, x_hbm, dy_hbm,
    gu_ref, gd_ref, x_ref, dy_ref, tab_ref, own_sem, send_sem, recv_sem,
):
    spot = Spot()
    mine = (up_ref, dn_ref)
    full = (gu_ref, gd_ref)
    first_p, first_m = {"fsdp": spot.owner(1, 0)}, {"fsdp": spot.owner(3, 0)}
    second_p, second_m = {"fsdp": spot.owner(0, 1)}, {"fsdp": spot.owner(0, 3)}
    other = {"fsdp": spot.sibling()}
    greet([first_p, first_m, second_p, second_m, other])
    mail = Mail(send_sem, recv_sem)
    me = spot.owner(0, 0)

    def held(i, j, h):
        return mine[h] if (i, j) == (0, 0) else full[h].at[spot.owner(i, j)]

    def place(i, j, h):
        return full[h].at[spot.owner(i, j)]

    def arrive(i, j, h, key, source):
        mail.wait(place(i, j, h), key, source)

    def share(i, j, h):
        mail.send(held(i, j, h), place(i, j, h), other, ("sib", i, j, h))

    def second(i, h):
        mail.send(held(i, 0, h), place(i, 0, h), second_p, ("sec", i, 3, h))
        mail.send(held(i, 0, h), place(i, 0, h), second_m, ("sec", i, 1, h))

    keeps = [
        pltpu.make_async_copy(src, dst, own_sem.at[n])
        for n, (src, dst) in enumerate((
            (up_ref, gu_ref.at[me]), (dn_ref, gd_ref.at[me])
        ))
    ]
    blocks = x_ref.shape[0]

    def cut(b, carry):
        at = pl.ds(pl.multiple_of(b * EDGE, EDGE), EDGE)
        pltpu.make_async_copy(x_hbm.at[:, at], x_ref.at[b], own_sem.at[2]).start()
        pltpu.make_async_copy(dy_hbm.at[:, at], dy_ref.at[b], own_sem.at[3]).start()
        return carry

    for h in (0, 1):
        mail.send(mine[h], place(0, 0, h), first_p, ("fst", 3, h))
        mail.send(mine[1 - h], place(0, 0, 1 - h), first_m, ("fst", 1, 1 - h))
    for h in (0, 1):
        second(0, h)
    for h in (0, 1):
        share(0, 0, h)
    for keep in keeps:
        keep.start()
    lax.fori_loop(0, blocks, cut, 0)
    slot_tables(rows_ref, cols_ref, counts, tab_ref)
    arrive(3, 0, 0, ("fst", 3, 0), first_m)
    mail.send(held(3, 0, 0), place(3, 0, 0), first_p, ("fst", 2, 0))
    arrive(1, 0, 1, ("fst", 1, 1), first_p)
    mail.send(held(1, 0, 1), place(1, 0, 1), first_m, ("fst", 2, 1))
    second(3, 0)
    second(1, 1)
    share(3, 0, 0)
    share(1, 0, 1)
    arrive(3, 0, 1, ("fst", 3, 1), first_m)
    second(3, 1)
    share(3, 0, 1)
    arrive(1, 0, 0, ("fst", 1, 0), first_p)
    second(1, 0)
    share(1, 0, 0)
    arrive(2, 0, 0, ("fst", 2, 0), first_m)
    second(2, 0)
    share(2, 0, 0)
    arrive(2, 0, 1, ("fst", 2, 1), first_p)
    second(2, 1)
    share(2, 0, 1)
    for i in (0, 3, 1, 2):
        arrive(i, 3, 0, ("sec", i, 3, 0), second_m)
        mail.send(held(i, 3, 0), place(i, 3, 0), second_p, ("sec", i, 2, 0))
        share(i, 3, 0)
        arrive(i, 1, 1, ("sec", i, 1, 1), second_p)
        mail.send(held(i, 1, 1), place(i, 1, 1), second_m, ("sec", i, 2, 1))
        share(i, 1, 1)
        arrive(i, 3, 1, ("sec", i, 3, 1), second_m)
        share(i, 3, 1)
        arrive(i, 1, 0, ("sec", i, 1, 0), second_p)
        share(i, 1, 0)
    for i in (0, 3, 1, 2):
        arrive(i, 2, 0, ("sec", i, 2, 0), second_m)
        share(i, 2, 0)
        arrive(i, 2, 1, ("sec", i, 2, 1), second_p)
        share(i, 2, 1)
    for i in range(RING):
        for j in range(RING):
            for h in (0, 1):
                mail.wait(full[h].at[spot.owner(i, j, 1 - spot.c)], ("sib", i, j, h), other)
    for keep in keeps:
        keep.wait()
    pltpu.make_async_copy(x_ref, x_ref, own_sem.at[2]).wait()
    pltpu.make_async_copy(dy_ref, dy_ref, own_sem.at[3]).wait()
    mail.finish()
    assert len(mail.sent) == len(mail.keys) == AG_COPIES


def gather_weights(rows, cols, counts, up, dn, x, dy):
    owners = 2 * RING * RING
    any_spec = pl.BlockSpec(memory_space=pltpu.HBM)
    vmem_spec = pl.BlockSpec(memory_space=pltpu.VMEM)
    full = pltpu.VMEM((owners,) + up.shape, up.dtype)
    cut = pltpu.VMEM((x.shape[1] // EDGE, x.shape[0], EDGE), x.dtype)
    return pl.pallas_call(
        gather_kernel,
        out_shape=(
            full, full, cut, cut,
            jax.ShapeDtypeStruct((8, SLOT_TOTAL), jnp.int32),
        ),
        in_specs=[vmem_spec] * 2 + [pl.BlockSpec(memory_space=pltpu.SMEM)] + [any_spec] * 4,
        out_specs=(vmem_spec,) * 5,
        scratch_shapes=[
            pltpu.SemaphoreType.DMA((4,)),
            pltpu.SemaphoreType.DMA((AG_COPIES,)),
            pltpu.SemaphoreType.DMA((AG_COPIES,)),
        ],
        compiler_params=pltpu.CompilerParams(
            collective_id=0, has_side_effects=True, vmem_limit_bytes=VM_K1
        ),
        name="gather_weights",
    )(rows.reshape(1, SLOT_TOTAL), cols.reshape(1, SLOT_TOTAL), counts,
      in_hbm(up), in_hbm(dn), in_hbm(x), in_hbm(dy))


NT = (((1,), (1,)), ((), ()))
TN = (((0,), (0,)), ((), ()))
NN = (((1,), (0,)), ((), ()))


def mm(a, b, dims):
    return lax.dot_general(a, b, dims, preferred_element_type=F32)


UNROLL = 4


def layer_kernel(
    rows, cols, tab, x, dy, up, dn, out_hbm, in_hbm, hid, pgr, out, inp, acc, sem
):
    row_blocks, tok = x.shape[:2]
    width = row_blocks * EDGE
    n_live = tab[LIVE, 0]
    steps = (n_live + UNROLL - 1) // UNROLL

    def block(b):
        return pl.ds(pl.multiple_of(b * EDGE, EDGE), EDGE)

    hid[DEAD] = jnp.zeros((tok, EDGE), BF16)
    pgr[DEAD] = jnp.zeros((tok, EDGE), BF16)

    def forward(step, carry):
        pre, back = acc[0], acc[1]
        for u in range(UNROLL):
            s = step * UNROLL + u
            k = tab[BY_COL, jnp.minimum(s, n_live - 1)]
            before = tab[BY_COL, jnp.clip(s - 1, 0, n_live - 1)]
            r = rows[k]
            first = jnp.logical_or(s == 0, cols[before] != cols[k])
            pre = jnp.where(first, 0.0, pre) + mm(x[r], up[k], NN)
            back = jnp.where(first, 0.0, back) + mm(dy[r], dn[k], NT)
            value, slope = gelu_parts(pre)
            to = jnp.where(s < n_live, s, DEAD + 1)
            hid[to] = value.astype(BF16)
            pgr[to] = (back * slope).astype(BF16)
        acc[0] = pre
        acc[1] = back
        return carry

    lax.fori_loop(0, steps, forward, 0)

    def clear(b, carry):
        out[:, block(b)] = jnp.zeros((tok, EDGE), BF16)
        inp[:, block(b)] = jnp.zeros((tok, EDGE), BF16)
        return carry

    lax.fori_loop(0, row_blocks, clear, 0)

    def put(b, carry):
        pltpu.make_async_copy(out.at[:, block(b)], out_hbm.at[:, block(b)], sem.at[0]).start()
        pltpu.make_async_copy(inp.at[:, block(b)], in_hbm.at[:, block(b)], sem.at[1]).start()
        return carry

    def backward(step, done):
        o, g = acc[0], acc[1]
        for u in range(UNROLL):
            t = step * UNROLL + u
            k = tab[BY_ROW, jnp.minimum(t, n_live - 1)]
            r = rows[k]
            before = tab[BY_ROW, jnp.clip(t - 1, 0, n_live - 1)]
            to = block(jnp.where(t < n_live, r, row_blocks))
            first = jnp.logical_or(t == 0, rows[before] != r)
            last = tab[LAST, k]
            o = jnp.where(first, 0.0, o) + mm(hid[last], dn[k], NN)
            g = jnp.where(first, 0.0, g) + mm(pgr[last], up[k], NT)
            out[:, to] = o.astype(BF16)
            inp[:, to] = g.astype(BF16)
        acc[0] = o
        acc[1] = g
        upto = rows[tab[BY_ROW, jnp.minimum((step + 1) * UNROLL - 1, n_live - 1)]]
        lax.fori_loop(done, upto, put, 0)
        return upto

    done = lax.fori_loop(0, steps, backward, 0)
    lax.fori_loop(done, row_blocks, put, 0)
    whole = pl.ds(0, width)
    pltpu.make_async_copy(out.at[:, whole], out_hbm, sem.at[0]).wait()
    pltpu.make_async_copy(inp.at[:, whole], in_hbm, sem.at[1]).wait()


def local_layer(rows, cols, tab, x, dy, up, dn):
    row_blocks, tok = x.shape[:2]
    width = row_blocks * EDGE
    any_spec = pl.BlockSpec(memory_space=pl.ANY)
    smem_spec = pl.BlockSpec(memory_space=pltpu.SMEM)
    vmem_spec = pl.BlockSpec(memory_space=pltpu.VMEM)
    kept = pltpu.VMEM((SLOT_TOTAL + 2, tok, EDGE), BF16)
    result = jax.ShapeDtypeStruct((tok, width), BF16)
    return pl.pallas_call(
        layer_kernel,
        out_shape=(result, result, kept, kept),
        in_specs=[smem_spec] * 3 + [vmem_spec] * 4,
        out_specs=(any_spec,) * 2 + (vmem_spec,) * 2,
        scratch_shapes=[
            pltpu.VMEM((tok, width + EDGE), BF16),
            pltpu.VMEM((tok, width + EDGE), BF16),
            pltpu.VMEM((2, tok, EDGE), F32),
            pltpu.SemaphoreType.DMA((2,)),
        ],
        compiler_params=pltpu.CompilerParams(vmem_limit_bytes=VM_K2),
        name="local_layer",
    )(
        rows, cols, tab, in_vmem(x), in_vmem(dy),
        in_vmem(up.reshape(SLOT_TOTAL, EDGE, EDGE)), in_vmem(dn.reshape(SLOT_TOTAL, EDGE, EDGE)),
    )


VM_K2 = 16 << 20


def in_hbm(array):
    return pltpu.with_memory_space_constraint(array, pltpu.HBM)


def in_vmem(array):
    return pltpu.with_memory_space_constraint(array, pltpu.VMEM)


RS_COPIES = 66
VM_K3 = 26 << 20


def scatter_kernel(
    scale, rows, tab, x, dy, hid, pgr, ug_ref, dg_ref,
    stage, own, sib, mid, got_m, got_p, r_bf, r_f32, mid2, fin_m, fin_p, zsend, zrecv,
    send_sem, recv_sem,
):
    spot = Spot()
    final = (ug_ref, dg_ref)
    first_p, first_m = {"fsdp": spot.owner(1, 0)}, {"fsdp": spot.owner(3, 0)}
    second_p, second_m = {"fsdp": spot.owner(0, 1)}, {"fsdp": spot.owner(0, 3)}
    other = {"fsdp": spot.sibling()}
    z_a = {"dp": spot.z + 1 - 2 * lax.rem(spot.z, 2)}
    z_b = {"dp": RING - 1 - spot.z}
    greet([first_p, first_m, second_p, second_m, other, z_a, z_b])
    mail = Mail(send_sem, recv_sem)

    def partial(owner, h, q):
        k = owner * SLOTS + q
        if h == 0:
            return mm(x[rows[k]], pgr[tab[LAST, k]], TN)
        return mm(hid[tab[LAST, k]], dy[rows[k]], TN)

    def give(j):
        def step(n, carry):
            i = turn(n)
            at = i * RING + j
            for h in (0, 1):
                for q in range(SLOTS):
                    stage[h, at, q] = partial(spot.owner(i, j, 1 - spot.c), h, q).astype(BF16)
                mail.send_at(stage.at[h, at], sib.at[h, at], other, 2 * at + h)
            return carry
        lax.fori_loop(0, RING, step, 0)

    def pair(i, j, h, then, *more):
        at = i * RING + j
        mail.wait_at(sib.at[h, at], other, 2 * at + h)
        for q in range(SLOTS):
            value = partial(spot.owner(i, j), h, q) + sib[h, at, q].astype(F32)
            for ref in more:
                value = value + ref[q].astype(F32)
            then(q, value)

    def keep(i, j, h, *more):
        at = i * RING + j

        def then(q, value):
            own[h, at, q] = value.astype(BF16)

        pair(i, j, h, then, *more)
        return own.at[h, at]

    base = 2 * RING * RING
    give(2)
    give(3)

    def far(n, carry):
        i = turn(n)
        mail.send_at(keep(i, 2, 0), mid.at[i, 0], second_p, base + i)
        mail.send_at(keep(i, 2, 1), mid.at[i, 1], second_m, base + RING + i)
        return carry

    lax.fori_loop(0, RING, far, 0)
    give(1)
    base += 2 * RING

    def near(n, carry):
        i = turn(n)
        mail.send_at(keep(i, 1, 1), got_m.at[i, 1], second_p, base + i)
        mail.send_at(keep(i, 3, 0), got_p.at[i, 0], second_m, base + RING + i)
        mail.wait_at(mid.at[i, 0], second_m, base - 2 * RING + i)
        mail.send_at(keep(i, 1, 0, mid.at[i, 0]), got_m.at[i, 0], second_p, base + 2 * RING + i)
        mail.wait_at(mid.at[i, 1], second_p, base - RING + i)
        mail.send_at(keep(i, 3, 1, mid.at[i, 1]), got_p.at[i, 1], second_m, base + 3 * RING + i)
        return carry

    lax.fori_loop(0, RING, near, 0)
    give(0)

    def ring_sum(i, h, then):
        mail.wait_at(got_m.at[i, h], second_m, base + (2 * RING, 0)[h] + i)
        mail.wait_at(got_p.at[i, h], second_p, base + (RING, 3 * RING)[h] + i)
        pair(i, 0, h, then, got_m.at[i, h], got_p.at[i, h])

    one = base + 4 * RING
    for n, (i, h, dst, target) in enumerate((
        (2, 0, mid2.at[0], first_p),
        (2, 1, mid2.at[1], first_m),
        (1, 1, fin_m.at[1], first_p),
        (3, 0, fin_p.at[0], first_m),
    )):
        def store(q, value):
            r_bf[n, q] = value.astype(BF16)

        ring_sum(i, h, store)
        mail.send_at(r_bf.at[n], dst, target, one + n)
    for n, (i, h, dst, target, source) in enumerate((
        (1, 0, fin_m.at[0], first_p, first_m),
        (3, 1, fin_p.at[1], first_m, first_p),
    )):
        def store(q, value):
            r_f32[n, q] = value

        ring_sum(i, h, store)
        mail.wait_at(mid2.at[h], source, one + h)
        r_bf[4 + n] = (r_f32[n] + mid2[h].astype(F32)).astype(BF16)
        mail.send_at(r_bf.at[4 + n], dst, target, one + 4 + n)
    for h in (0, 1):
        def store(q, value):
            r_f32[h, q] = value

        ring_sum(0, h, store)
    plane = one + 6
    for h in (0, 1):
        mail.wait_at(fin_m.at[h], first_m, one + (4, 2)[h])
        mail.wait_at(fin_p.at[h], first_p, one + (3, 5)[h])
        value = r_f32[h] + fin_m[h].astype(F32) + fin_p[h].astype(F32)
        zsend[0, h] = value.astype(BF16)
        mail.send_at(zsend.at[0, h], zrecv.at[0, h], (z_a, z_b)[h], plane + h)
    for h in (0, 1):
        mail.wait_at(zrecv.at[0, h], (z_a, z_b)[h], plane + h)
        value = zsend[0, h].astype(F32) + zrecv[0, h].astype(F32)
        zsend[1, h] = value.astype(BF16)
        mail.send_at(zsend.at[1, h], zrecv.at[1, h], (z_b, z_a)[h], plane + 2 + h)
    for h in (0, 1):
        mail.wait_at(zrecv.at[1, h], (z_b, z_a)[h], plane + 2 + h)
        value = zsend[1, h].astype(F32) + zrecv[1, h].astype(F32)
        final[h][...] = value * scale

    def sent(n, carry):
        mail.sent_at(stage.at[0, 0], other, n)
        return carry

    lax.fori_loop(0, RS_COPIES, sent, 0)


def turn(n):
    return lax.rem(2 + n * (n + 1) // 2, RING)


def scatter_grads(rows, tab, x, dy, hid, pgr, scale):
    piece = (SLOTS, EDGE, EDGE)
    grad = jax.ShapeDtypeStruct(piece, F32)
    vmem = pl.BlockSpec(memory_space=pltpu.VMEM)
    smem = pl.BlockSpec(memory_space=pltpu.SMEM)
    return pl.pallas_call(
        functools.partial(scatter_kernel, scale),
        out_shape=(grad, grad),
        in_specs=[smem] * 2 + [vmem] * 4,
        out_specs=(vmem, vmem),
        scratch_shapes=[
            pltpu.VMEM((2, RING * RING) + piece, BF16),
            pltpu.VMEM((2, RING * RING) + piece, BF16),
            pltpu.VMEM((2, RING * RING) + piece, BF16),
            pltpu.VMEM((RING, 2) + piece, BF16),
            pltpu.VMEM((RING, 2) + piece, BF16),
            pltpu.VMEM((RING, 2) + piece, BF16),
            pltpu.VMEM((6,) + piece, BF16),
            pltpu.VMEM((2,) + piece, F32),
            pltpu.VMEM((2,) + piece, BF16),
            pltpu.VMEM((2,) + piece, BF16),
            pltpu.VMEM((2,) + piece, BF16),
            pltpu.VMEM((2, 2) + piece, BF16),
            pltpu.VMEM((2, 2) + piece, BF16),
            pltpu.SemaphoreType.DMA((RS_COPIES,)),
            pltpu.SemaphoreType.DMA((RS_COPIES,)),
        ],
        compiler_params=pltpu.CompilerParams(
            collective_id=1, has_side_effects=True, vmem_limit_bytes=VM_K3
        ),
        name="scatter_grads",
    )(rows, tab, in_vmem(x), in_vmem(dy), in_vmem(hid), in_vmem(pgr))


def on_device(tokens, cotangent, up_w, dn_w, block_rows, block_cols, owner_counts):
    devices = lax.axis_size("dp") * lax.axis_size("fsdp")
    scale = 1.0 / math.sqrt(tokens.shape[0] * devices)
    up_full, dn_full, x, dy, tab = gather_weights(
        block_rows, block_cols, owner_counts, up_w, dn_w, tokens, cotangent
    )
    output, input_grad, hid, pgr = local_layer(
        block_rows, block_cols, tab, x, dy, up_full, dn_full
    )
    up_grad, down_grad = scatter_grads(block_rows, tab, x, dy, hid, pgr, scale)
    return output, input_grad, up_grad, down_grad


def solution(mesh):
    in_specs = (
        P(("dp", "fsdp"), None),
        P(("dp", "fsdp"), None),
        P("fsdp", None, None),
        P("fsdp", None, None),
        P(),
        P(),
        P(),
    )
    out_specs = (
        P(("dp", "fsdp"), None),
        P(("dp", "fsdp"), None),
        P("fsdp", None, None),
        P("fsdp", None, None),
    )
    return jax.shard_map(
        on_device, mesh=mesh, in_specs=in_specs, out_specs=out_specs, check_vma=False
    )
```

```python
import functools
import math

import jax
import jax.numpy as jnp
from jax import lax
from jax.experimental import pallas as pl
from jax.experimental.pallas import tpu as pltpu
from jax.sharding import PartitionSpec as P

EDGE = 128
SLOTS = 4
RING = 4
MESH_ID = pl.DeviceIdType.MESH
BF16 = jnp.bfloat16
F32 = jnp.float32

gelu_scale = 0.7978845608028654
cubic_coef = 0.044715


def gelu_parts(values):
    square = values * values
    tanh_val = jnp.tanh(values * (gelu_scale + gelu_scale * cubic_coef * square))
    half = 0.5 * values
    gelu_value = half + half * tanh_val
    gelu_slope = (0.5 + 0.5 * tanh_val) + half * (1.0 - tanh_val * tanh_val) * (
        gelu_scale + 3.0 * gelu_scale * cubic_coef * square
    )
    return gelu_value, gelu_slope


class Spot:
    def __init__(self):
        me = lax.axis_index("fsdp")
        self.z = lax.axis_index("dp")
        self.c = lax.rem(me, 2)
        self.y = lax.rem(me // 2, RING)
        self.x = me // (2 * RING)

    def owner(self, i, j, c=None):
        c = self.c if c is None else c
        x = lax.rem(self.x + i * (1 - c) + j * c, RING)
        y = lax.rem(self.y + i * c + j * (1 - c), RING)
        return (x * RING + y) * 2 + c

    def sibling(self):
        return (self.x * RING + self.y) * 2 + (1 - self.c)


def greet(targets, meanwhile=None):
    barrier = pltpu.get_barrier_semaphore()
    for target in targets:
        pl.semaphore_signal(barrier, inc=1, device_id=target, device_id_type=MESH_ID)
    if meanwhile is not None:
        meanwhile()
    pl.semaphore_wait(barrier, len(targets))


class Mail:
    def __init__(self, send_sem, recv_sem):
        self.send_sem, self.recv_sem = send_sem, recv_sem
        self.keys, self.sent = {}, []

    def slot(self, key):
        return self.keys.setdefault(key, len(self.keys))

    def send(self, src, dst, target, key):
        copy = pltpu.make_async_remote_copy(
            src_ref=src,
            dst_ref=dst,
            send_sem=self.send_sem.at[len(self.sent)],
            recv_sem=self.recv_sem.at[self.slot(key)],
            device_id=target,
            device_id_type=MESH_ID,
        )
        copy.start()
        self.sent.append(copy)

    def wait(self, dst, key, target):
        pltpu.make_async_remote_copy(
            src_ref=dst,
            dst_ref=dst,
            send_sem=self.send_sem.at[0],
            recv_sem=self.recv_sem.at[self.slot(key)],
            device_id=target,
            device_id_type=MESH_ID,
        ).wait_recv()

    def finish(self):
        for copy in self.sent:
            copy.wait_send()

    def copy_at(self, src, dst, target, n):
        return pltpu.make_async_remote_copy(
            src_ref=src,
            dst_ref=dst,
            send_sem=self.send_sem.at[n],
            recv_sem=self.recv_sem.at[n],
            device_id=target,
            device_id_type=MESH_ID,
        )

    def send_at(self, src, dst, target, n):
        self.copy_at(src, dst, target, n).start()

    def wait_at(self, dst, target, n):
        self.copy_at(dst, dst, target, n).wait_recv()

    def sent_at(self, src, target, n):
        self.copy_at(src, src, target, n).wait_send()


VM_K1 = 8 << 20
AG_COPIES = 62
SLOT_TOTAL = 128
DEAD = SLOT_TOTAL
BY_COL, BY_ROW, LAST, LIVE = 0, 1, 2, 3


def slot_tables(rows_ref, cols_ref, counts, tab_ref):
    n = SLOT_TOTAL
    lane = lax.broadcasted_iota(jnp.int32, (n, n), 1)
    sub = lax.broadcasted_iota(jnp.int32, (n, n), 0)
    lane_owner = lax.broadcasted_iota(jnp.int32, (8, n), 1) // SLOTS
    held = jnp.zeros((8, n), jnp.int32)
    for o in range(n // SLOTS):
        held = jnp.where(lane_owner == o, counts[o], held)
    lane_f, sub_f = lane.astype(F32), sub.astype(F32)

    def spread(row):
        across = jnp.broadcast_to(row.astype(F32), (n, n))
        return across, across.T

    held_l, held_s = spread(held[0:1])
    slot_l = lax.rem(lane, SLOTS).astype(F32)
    slot_s = lax.rem(sub, SLOTS).astype(F32)
    live_l = jnp.where(slot_l < held_l, 1.0, 0.0)
    live_s = jnp.where(slot_s < held_s, 1.0, 0.0)

    def order(key_l, key_s):
        tie = jnp.where(key_l == key_s, jnp.where(lane < sub, live_l, 0.0), 0.0)
        rank = jnp.sum(jnp.where(key_l < key_s, live_l, tie), axis=1, keepdims=True)
        hit = jnp.where(rank == lane_f, live_s, 0.0)
        return jnp.sum(hit * sub_f, axis=0, keepdims=True)

    col_l, col_s = spread(cols_ref[...])
    row_l, row_s = spread(rows_ref[...])
    upto = jnp.sum(jnp.where(col_s <= col_l, live_s, 0.0), axis=0, keepdims=True)
    last = jnp.where(live_l[0:1] > 0.5, upto - 1.0, float(DEAD))
    number = jnp.sum(live_s, axis=0, keepdims=True)
    for at, row in (
        (BY_COL, order(col_l, col_s)), (BY_ROW, order(row_l, row_s)), (LAST, last), (LIVE, number)
    ):
        tab_ref[at:at + 1, :] = row.astype(jnp.int32)


def gather_kernel(
    rows_hbm, cols_hbm, counts_hbm, up_ref, dn_ref, x_hbm, dy_hbm,
    gu_ref, gd_ref, x_ref, dy_ref, tab_ref, rows_ref, cols_ref, counts,
    own_sem, send_sem, recv_sem,
):
    spot = Spot()
    mine = (up_ref, dn_ref)
    full = (gu_ref, gd_ref)
    first_p, first_m = {"fsdp": spot.owner(1, 0)}, {"fsdp": spot.owner(3, 0)}
    second_p, second_m = {"fsdp": spot.owner(0, 1)}, {"fsdp": spot.owner(0, 3)}
    other = {"fsdp": spot.sibling()}
    mail = Mail(send_sem, recv_sem)
    me = spot.owner(0, 0)

    def held(i, j, h):
        return mine[h] if (i, j) == (0, 0) else full[h].at[spot.owner(i, j)]

    def place(i, j, h):
        return full[h].at[spot.owner(i, j)]

    def arrive(i, j, h, key, source):
        mail.wait(place(i, j, h), key, source)

    def share(i, j, h):
        mail.send(held(i, j, h), place(i, j, h), other, ("sib", i, j, h))

    def second(i, h):
        mail.send(held(i, 0, h), place(i, 0, h), second_p, ("sec", i, 3, h))
        mail.send(held(i, 0, h), place(i, 0, h), second_m, ("sec", i, 1, h))

    keeps = [
        pltpu.make_async_copy(src, dst, own_sem.at[n])
        for n, (src, dst) in enumerate((
            (up_ref, gu_ref.at[me]), (dn_ref, gd_ref.at[me]),
            (x_ref, x_ref), (dy_ref, dy_ref),
            (rows_hbm, rows_ref), (cols_hbm, cols_ref), (counts_hbm, counts),
        ))
    ]
    blocks = x_ref.shape[0]

    def cut(b, carry):
        at = pl.ds(pl.multiple_of(b * EDGE, EDGE), EDGE)
        pltpu.make_async_copy(x_hbm.at[:, at], x_ref.at[b], own_sem.at[2]).start()
        pltpu.make_async_copy(dy_hbm.at[:, at], dy_ref.at[b], own_sem.at[3]).start()
        return carry

    def load():
        for n in (4, 5, 6, 0, 1):
            keeps[n].start()
        lax.fori_loop(0, blocks, cut, 0)

    greet([first_p, first_m, second_p, second_m, other], load)
    for h in (0, 1):
        mail.send(mine[h], place(0, 0, h), first_p, ("fst", 3, h))
        mail.send(mine[1 - h], place(0, 0, 1 - h), first_m, ("fst", 1, 1 - h))
    for h in (0, 1):
        second(0, h)
    for h in (0, 1):
        share(0, 0, h)
    for n in (4, 5, 6):
        keeps[n].wait()
    slot_tables(rows_ref, cols_ref, counts, tab_ref)
    arrive(3, 0, 0, ("fst", 3, 0), first_m)
    mail.send(held(3, 0, 0), place(3, 0, 0), first_p, ("fst", 2, 0))
    arrive(1, 0, 1, ("fst", 1, 1), first_p)
    mail.send(held(1, 0, 1), place(1, 0, 1), first_m, ("fst", 2, 1))
    second(3, 0)
    second(1, 1)
    share(3, 0, 0)
    share(1, 0, 1)
    arrive(3, 0, 1, ("fst", 3, 1), first_m)
    second(3, 1)
    share(3, 0, 1)
    arrive(1, 0, 0, ("fst", 1, 0), first_p)
    second(1, 0)
    share(1, 0, 0)
    arrive(2, 0, 0, ("fst", 2, 0), first_m)
    second(2, 0)
    share(2, 0, 0)
    arrive(2, 0, 1, ("fst", 2, 1), first_p)
    second(2, 1)
    share(2, 0, 1)
    for i in (0, 3, 1, 2):
        arrive(i, 3, 0, ("sec", i, 3, 0), second_m)
        mail.send(held(i, 3, 0), place(i, 3, 0), second_p, ("sec", i, 2, 0))
        share(i, 3, 0)
        arrive(i, 1, 1, ("sec", i, 1, 1), second_p)
        mail.send(held(i, 1, 1), place(i, 1, 1), second_m, ("sec", i, 2, 1))
        share(i, 1, 1)
        arrive(i, 3, 1, ("sec", i, 3, 1), second_m)
        share(i, 3, 1)
        arrive(i, 1, 0, ("sec", i, 1, 0), second_p)
        share(i, 1, 0)
    for i in (0, 3, 1, 2):
        arrive(i, 2, 0, ("sec", i, 2, 0), second_m)
        share(i, 2, 0)
        arrive(i, 2, 1, ("sec", i, 2, 1), second_p)
        share(i, 2, 1)
    for i in range(RING):
        for j in range(RING):
            for h in (0, 1):
                mail.wait(full[h].at[spot.owner(i, j, 1 - spot.c)], ("sib", i, j, h), other)
    for n in range(4):
        keeps[n].wait()
    mail.finish()
    assert len(mail.sent) == len(mail.keys) == AG_COPIES


def gather_weights(rows, cols, counts, up, dn, x, dy):
    owners = 2 * RING * RING
    any_spec = pl.BlockSpec(memory_space=pltpu.HBM)
    vmem_spec = pl.BlockSpec(memory_space=pltpu.VMEM)
    full = pltpu.VMEM((owners,) + up.shape, up.dtype)
    cut = pltpu.VMEM((x.shape[1] // EDGE, x.shape[0], EDGE), x.dtype)
    return pl.pallas_call(
        gather_kernel,
        out_shape=(
            full, full, cut, cut,
            jax.ShapeDtypeStruct((8, SLOT_TOTAL), jnp.int32),
        ),
        in_specs=[any_spec] * 7,
        out_specs=(vmem_spec,) * 5,
        scratch_shapes=[
            pltpu.VMEM((1, SLOT_TOTAL), jnp.int32),
            pltpu.VMEM((1, SLOT_TOTAL), jnp.int32),
            pltpu.SMEM(counts.shape, jnp.int32),
            pltpu.SemaphoreType.DMA((7,)),
            pltpu.SemaphoreType.DMA((AG_COPIES,)),
            pltpu.SemaphoreType.DMA((AG_COPIES,)),
        ],
        compiler_params=pltpu.CompilerParams(
            collective_id=0, has_side_effects=True, vmem_limit_bytes=VM_K1
        ),
        name="gather_weights",
    )(
        in_hbm(rows.reshape(1, SLOT_TOTAL)), in_hbm(cols.reshape(1, SLOT_TOTAL)), in_hbm(counts),
        in_hbm(up), in_hbm(dn), in_hbm(x), in_hbm(dy),
    )


NT = (((1,), (1,)), ((), ()))
TN = (((0,), (0,)), ((), ()))
NN = (((1,), (0,)), ((), ()))


def mm(a, b, dims):
    return lax.dot_general(a, b, dims, preferred_element_type=F32)


UNROLL = 4


def layer_kernel(
    rows, cols, tab, x, dy, up, dn, out_hbm, in_hbm, hid, pgr, out, inp, acc, sem
):
    row_blocks, tok = x.shape[:2]
    width = row_blocks * EDGE
    n_live = tab[LIVE, 0]
    steps = (n_live + UNROLL - 1) // UNROLL

    def block(b):
        return pl.ds(pl.multiple_of(b * EDGE, EDGE), EDGE)

    hid[DEAD] = jnp.zeros((tok, EDGE), BF16)
    pgr[DEAD] = jnp.zeros((tok, EDGE), BF16)

    def forward(step, carry):
        pre, back = acc[0], acc[1]
        for u in range(UNROLL):
            s = step * UNROLL + u
            k = tab[BY_COL, jnp.minimum(s, n_live - 1)]
            before = tab[BY_COL, jnp.clip(s - 1, 0, n_live - 1)]
            r = rows[k]
            first = jnp.logical_or(s == 0, cols[before] != cols[k])
            pre = jnp.where(first, 0.0, pre) + mm(x[r], up[k], NN)
            back = jnp.where(first, 0.0, back) + mm(dy[r], dn[k], NT)
            value, slope = gelu_parts(pre)
            to = jnp.where(s < n_live, s, DEAD + 1)
            hid[to] = value.astype(BF16)
            pgr[to] = (back * slope).astype(BF16)
        acc[0] = pre
        acc[1] = back
        return carry

    lax.fori_loop(0, steps, forward, 0)

    def clear(b, carry):
        out[:, block(b)] = jnp.zeros((tok, EDGE), BF16)
        inp[:, block(b)] = jnp.zeros((tok, EDGE), BF16)
        return carry

    lax.fori_loop(0, row_blocks, clear, 0)

    def put(b, carry):
        pltpu.make_async_copy(out.at[:, block(b)], out_hbm.at[:, block(b)], sem.at[0]).start()
        pltpu.make_async_copy(inp.at[:, block(b)], in_hbm.at[:, block(b)], sem.at[1]).start()
        return carry

    def backward(step, done):
        o, g = acc[0], acc[1]
        for u in range(UNROLL):
            t = step * UNROLL + u
            k = tab[BY_ROW, jnp.minimum(t, n_live - 1)]
            r = rows[k]
            before = tab[BY_ROW, jnp.clip(t - 1, 0, n_live - 1)]
            to = block(jnp.where(t < n_live, r, row_blocks))
            first = jnp.logical_or(t == 0, rows[before] != r)
            last = tab[LAST, k]
            o = jnp.where(first, 0.0, o) + mm(hid[last], dn[k], NN)
            g = jnp.where(first, 0.0, g) + mm(pgr[last], up[k], NT)
            out[:, to] = o.astype(BF16)
            inp[:, to] = g.astype(BF16)
        acc[0] = o
        acc[1] = g
        upto = rows[tab[BY_ROW, jnp.minimum((step + 1) * UNROLL - 1, n_live - 1)]]
        lax.fori_loop(done, upto, put, 0)
        return upto

    done = lax.fori_loop(0, steps, backward, 0)
    lax.fori_loop(done, row_blocks, put, 0)
    whole = pl.ds(0, width)
    pltpu.make_async_copy(out.at[:, whole], out_hbm, sem.at[0]).wait()
    pltpu.make_async_copy(inp.at[:, whole], in_hbm, sem.at[1]).wait()


def local_layer(rows, cols, tab, x, dy, up, dn):
    row_blocks, tok = x.shape[:2]
    width = row_blocks * EDGE
    any_spec = pl.BlockSpec(memory_space=pl.ANY)
    smem_spec = pl.BlockSpec(memory_space=pltpu.SMEM)
    vmem_spec = pl.BlockSpec(memory_space=pltpu.VMEM)
    kept = pltpu.VMEM((SLOT_TOTAL + 2, tok, EDGE), BF16)
    result = jax.ShapeDtypeStruct((tok, width), BF16)
    return pl.pallas_call(
        layer_kernel,
        out_shape=(result, result, kept, kept),
        in_specs=[smem_spec] * 3 + [vmem_spec] * 4,
        out_specs=(any_spec,) * 2 + (vmem_spec,) * 2,
        scratch_shapes=[
            pltpu.VMEM((tok, width + EDGE), BF16),
            pltpu.VMEM((tok, width + EDGE), BF16),
            pltpu.VMEM((2, tok, EDGE), F32),
            pltpu.SemaphoreType.DMA((2,)),
        ],
        compiler_params=pltpu.CompilerParams(vmem_limit_bytes=VM_K2),
        name="local_layer",
    )(
        rows, cols, tab, in_vmem(x), in_vmem(dy),
        in_vmem(up.reshape(SLOT_TOTAL, EDGE, EDGE)), in_vmem(dn.reshape(SLOT_TOTAL, EDGE, EDGE)),
    )


VM_K2 = 16 << 20


def in_hbm(array):
    return pltpu.with_memory_space_constraint(array, pltpu.HBM)


def in_vmem(array):
    return pltpu.with_memory_space_constraint(array, pltpu.VMEM)


RS_COPIES = 50
VM_K3 = 26 << 20


def scatter_kernel(
    scale, rows, tab, x, dy, hid, pgr, ug_ref, dg_ref,
    stage, own, sib, mid, got_m, got_p, r_own, r_bf, r_f32, mid2, fin_m, fin_p, zsend, zrecv,
    send_sem, recv_sem,
):
    spot = Spot()
    final = (ug_ref, dg_ref)
    first_p, first_m = {"fsdp": spot.owner(1, 0)}, {"fsdp": spot.owner(3, 0)}
    second_p, second_m = {"fsdp": spot.owner(0, 1)}, {"fsdp": spot.owner(0, 3)}
    other = {"fsdp": spot.sibling()}
    z_a = {"dp": spot.z + 1 - 2 * lax.rem(spot.z, 2)}
    z_b = {"dp": RING - 1 - spot.z}
    mail = Mail(send_sem, recv_sem)

    def partial(owner, h, q):
        k = owner * SLOTS + q
        if h == 0:
            return mm(x[rows[k]], pgr[tab[LAST, k]], TN)
        return mm(hid[tab[LAST, k]], dy[rows[k]], TN)

    def make(i, j):
        at = i * RING + j
        for h in (0, 1):
            for q in range(SLOTS):
                stage[at, h, q] = partial(spot.owner(i, j, 1 - spot.c), h, q).astype(BF16)

    def give(i, j):
        at = i * RING + j
        mail.send_at(stage.at[at], sib.at[at], other, at)

    def given(i, j):
        at = i * RING + j
        mail.wait_at(sib.at[at], other, at)

    def keep(i, j, h, *more):
        at = i * RING + j
        for q in range(SLOTS):
            value = partial(spot.owner(i, j), h, q) + sib[at, h, q].astype(F32)
            for ref in more:
                value = value + ref[q].astype(F32)
            own[at, h, q] = value.astype(BF16)
        return own.at[at, h]

    mids = RING * RING
    base = mids + 2 * RING
    one = base + 4 * RING

    def turns(*acts):
        def step(n, carry):
            for act in acts:
                act(turn(n))
            return carry
        return step

    def make_give(j):
        def act(i):
            make(i, j)
            give(i, j)
        return act

    def far(i):
        given(i, 2)
        mail.send_at(keep(i, 2, 0), mid.at[i, 0], second_p, mids + i)
        mail.send_at(keep(i, 2, 1), mid.at[i, 1], second_m, mids + RING + i)

    def near(i):
        given(i, 1)
        mail.send_at(keep(i, 1, 1), got_m.at[i, 1], second_p, base + i)
        given(i, 3)
        mail.send_at(keep(i, 3, 0), got_p.at[i, 0], second_m, base + RING + i)
        mail.wait_at(mid.at[i, 0], second_m, mids + i)
        mail.send_at(keep(i, 1, 0, mid.at[i, 0]), got_m.at[i, 0], second_p, base + 2 * RING + i)
        mail.wait_at(mid.at[i, 1], second_p, mids + RING + i)
        mail.send_at(keep(i, 3, 1, mid.at[i, 1]), got_p.at[i, 1], second_m, base + 3 * RING + i)

    def stay(i):
        given(i, 0)
        at = i * RING
        for h in (0, 1):
            for q in range(SLOTS):
                r_own[i, h, q] = partial(spot.owner(i, 0), h, q) + sib[at, h, q].astype(F32)

    def ring_sum(i, h):
        mail.wait_at(got_m.at[i, h], second_m, base + (2 * RING, 0)[h] + i)
        mail.wait_at(got_p.at[i, h], second_p, base + (RING, 3 * RING)[h] + i)
        return r_own[i, h] + got_m[i, h].astype(F32) + got_p[i, h].astype(F32)

    def pass_on(n, i, h, dst, target):
        r_bf[n] = ring_sum(i, h).astype(BF16)
        mail.send_at(r_bf.at[n], dst.at[h], target, one + n)

    def add_on(n, i, h, dst, target):
        value = ring_sum(i, h)
        mail.wait_at(mid2.at[h], (first_m, first_p)[h], one + h)
        r_bf[4 + n] = (value + mid2[h].astype(F32)).astype(BF16)
        mail.send_at(r_bf.at[4 + n], dst.at[h], target, one + 4 + n)

    greet(
        [first_p, first_m, second_p, second_m, other, z_a, z_b],
        lambda: lax.fori_loop(0, RING, turns(lambda i: make(i, 2)), 0),
    )
    lax.fori_loop(0, 4, turns(lambda i: give(i, 2)), 0)
    lax.fori_loop(0, 4, turns(far, make_give(3), make_give(1)), 0)
    lax.fori_loop(0, 4, turns(near, make_give(0)), 0)
    lax.fori_loop(0, 4, turns(stay), 0)
    pass_on(0, 2, 0, mid2, first_p)
    pass_on(1, 2, 1, mid2, first_m)
    pass_on(2, 1, 1, fin_m, first_p)
    pass_on(3, 3, 0, fin_p, first_m)
    add_on(0, 1, 0, fin_m, first_p)
    add_on(1, 3, 1, fin_p, first_m)
    for h in (0, 1):
        r_f32[h] = ring_sum(0, h)
    plane = one + 6
    for h in (0, 1):
        mail.wait_at(fin_m.at[h], first_m, one + (4, 2)[h])
        mail.wait_at(fin_p.at[h], first_p, one + (3, 5)[h])
        value = r_f32[h] + fin_m[h].astype(F32) + fin_p[h].astype(F32)
        zsend[0, h] = value.astype(BF16)
        mail.send_at(zsend.at[0, h], zrecv.at[0, h], (z_a, z_b)[h], plane + h)
    for h in (0, 1):
        mail.wait_at(zrecv.at[0, h], (z_a, z_b)[h], plane + h)
        value = zsend[0, h].astype(F32) + zrecv[0, h].astype(F32)
        zsend[1, h] = value.astype(BF16)
        mail.send_at(zsend.at[1, h], zrecv.at[1, h], (z_b, z_a)[h], plane + 2 + h)
    for h in (0, 1):
        mail.wait_at(zrecv.at[1, h], (z_b, z_a)[h], plane + 2 + h)
        value = zsend[1, h].astype(F32) + zrecv[1, h].astype(F32)
        final[h][...] = value * scale

    def sent(n, carry):
        mail.sent_at(mid.at[0, 0], other, n)
        return carry

    def sent_pair(n, carry):
        mail.sent_at(stage.at[0], other, n)
        return carry

    lax.fori_loop(0, mids, sent_pair, 0)
    lax.fori_loop(mids, RS_COPIES, sent, 0)


def turn(n):
    return lax.rem(2 + n * (n + 1) // 2, RING)


def scatter_grads(rows, tab, x, dy, hid, pgr, scale):
    piece = (SLOTS, EDGE, EDGE)
    grad = jax.ShapeDtypeStruct(piece, F32)
    vmem = pl.BlockSpec(memory_space=pltpu.VMEM)
    smem = pl.BlockSpec(memory_space=pltpu.SMEM)
    return pl.pallas_call(
        functools.partial(scatter_kernel, scale),
        out_shape=(grad, grad),
        in_specs=[smem] * 2 + [vmem] * 4,
        out_specs=(vmem, vmem),
        scratch_shapes=[
            pltpu.VMEM((RING * RING, 2) + piece, BF16),
            pltpu.VMEM((RING * RING, 2) + piece, BF16),
            pltpu.VMEM((RING * RING, 2) + piece, BF16),
            pltpu.VMEM((RING, 2) + piece, BF16),
            pltpu.VMEM((RING, 2) + piece, BF16),
            pltpu.VMEM((RING, 2) + piece, BF16),
            pltpu.VMEM((RING, 2) + piece, F32),
            pltpu.VMEM((6,) + piece, BF16),
            pltpu.VMEM((2,) + piece, F32),
            pltpu.VMEM((2,) + piece, BF16),
            pltpu.VMEM((2,) + piece, BF16),
            pltpu.VMEM((2,) + piece, BF16),
            pltpu.VMEM((2, 2) + piece, BF16),
            pltpu.VMEM((2, 2) + piece, BF16),
            pltpu.SemaphoreType.DMA((RS_COPIES,)),
            pltpu.SemaphoreType.DMA((RS_COPIES,)),
        ],
        compiler_params=pltpu.CompilerParams(
            collective_id=1, has_side_effects=True, vmem_limit_bytes=VM_K3
        ),
        name="scatter_grads",
    )(rows, tab, in_vmem(x), in_vmem(dy), in_vmem(hid), in_vmem(pgr))


def on_device(tokens, cotangent, up_w, dn_w, block_rows, block_cols, owner_counts):
    devices = lax.axis_size("dp") * lax.axis_size("fsdp")
    scale = 1.0 / math.sqrt(tokens.shape[0] * devices)
    up_full, dn_full, x, dy, tab = gather_weights(
        block_rows, block_cols, owner_counts, up_w, dn_w, tokens, cotangent
    )
    output, input_grad, hid, pgr = local_layer(
        block_rows, block_cols, tab, x, dy, up_full, dn_full
    )
    up_grad, down_grad = scatter_grads(block_rows, tab, x, dy, hid, pgr, scale)
    return output, input_grad, up_grad, down_grad


def solution(mesh):
    in_specs = (
        P(("dp", "fsdp"), None),
        P(("dp", "fsdp"), None),
        P("fsdp", None, None),
        P("fsdp", None, None),
        P(),
        P(),
        P(),
    )
    out_specs = (
        P(("dp", "fsdp"), None),
        P(("dp", "fsdp"), None),
        P("fsdp", None, None),
        P("fsdp", None, None),
    )
    return jax.shard_map(
        on_device, mesh=mesh, in_specs=in_specs, out_specs=out_specs, check_vma=False
    )
```

```python
import functools
import math

import jax
import jax.numpy as jnp
from jax import lax
from jax.experimental import pallas as pl
from jax.experimental.pallas import tpu as pltpu
from jax.sharding import PartitionSpec as P

EDGE = 128
SLOTS = 4
RING = 4
MESH_ID = pl.DeviceIdType.MESH
BF16 = jnp.bfloat16
F32 = jnp.float32

gelu_scale = 0.7978845608028654
cubic_coef = 0.044715


def gelu_parts(values):
    square = values * values
    tanh_val = jnp.tanh(values * (gelu_scale + gelu_scale * cubic_coef * square))
    half = 0.5 * values
    gelu_value = half + half * tanh_val
    gelu_slope = (0.5 + 0.5 * tanh_val) + half * (1.0 - tanh_val * tanh_val) * (
        gelu_scale + 3.0 * gelu_scale * cubic_coef * square
    )
    return gelu_value, gelu_slope


class Spot:
    def __init__(self):
        me = lax.axis_index("fsdp")
        self.z = lax.axis_index("dp")
        self.c = lax.rem(me, 2)
        self.y = lax.rem(me // 2, RING)
        self.x = me // (2 * RING)

    def owner(self, i, j, c=None):
        c = self.c if c is None else c
        x = lax.rem(self.x + i * (1 - c) + j * c, RING)
        y = lax.rem(self.y + i * c + j * (1 - c), RING)
        return (x * RING + y) * 2 + c

    def sibling(self):
        return (self.x * RING + self.y) * 2 + (1 - self.c)


def greet(targets, meanwhile=None):
    barrier = pltpu.get_barrier_semaphore()
    for target in targets:
        pl.semaphore_signal(barrier, inc=1, device_id=target, device_id_type=MESH_ID)
    if meanwhile is not None:
        meanwhile()
    pl.semaphore_wait(barrier, len(targets))


class Mail:
    def __init__(self, send_sem, recv_sem):
        self.send_sem, self.recv_sem = send_sem, recv_sem
        self.keys, self.sent = {}, 0

    def copy(self, src, dst, target, n, lane):
        return pltpu.make_async_remote_copy(
            src_ref=src,
            dst_ref=dst,
            send_sem=self.send_sem.at[lane],
            recv_sem=self.recv_sem.at[n],
            device_id=target,
            device_id_type=MESH_ID,
        )

    def slot(self, key):
        return key if isinstance(key, int) else self.keys.setdefault(key, 2 + len(self.keys))

    def send(self, src, dst, target, key, lane=0):
        self.copy(src, dst, target, self.slot(key), lane).start()
        self.sent += 1

    def wait(self, dst, key, target):
        self.copy(dst, dst, target, self.slot(key), 0).wait_recv()

    def send_at(self, src, dst, target, n, lane):
        self.copy(src, dst, target, n, lane).start()

    def wait_at(self, dst, target, n):
        self.copy(dst, dst, target, n, 0).wait_recv()

    def sent_all(self, like, target, lane):
        self.copy(like, like, target, 0, lane).wait_send()


VM_K1 = 8 << 20
RING_COPIES = 30
SLOT_TOTAL = 128
DEAD = SLOT_TOTAL
BY_COL, BY_ROW, LAST, LIVE = 0, 1, 2, 3


def slot_tables(rows_ref, cols_ref, counts, tab_ref):
    n = SLOT_TOTAL
    lane = lax.broadcasted_iota(jnp.int32, (n, n), 1)
    sub = lax.broadcasted_iota(jnp.int32, (n, n), 0)
    lane_owner = lax.broadcasted_iota(jnp.int32, (8, n), 1) // SLOTS
    held = jnp.zeros((8, n), jnp.int32)
    for o in range(n // SLOTS):
        held = jnp.where(lane_owner == o, counts[o], held)
    lane_f, sub_f = lane.astype(F32), sub.astype(F32)

    def spread(row):
        across = jnp.broadcast_to(row.astype(F32), (n, n))
        return across, across.T

    held_l, held_s = spread(held[0:1])
    slot_l = lax.rem(lane, SLOTS).astype(F32)
    slot_s = lax.rem(sub, SLOTS).astype(F32)
    live_l = jnp.where(slot_l < held_l, 1.0, 0.0)
    live_s = jnp.where(slot_s < held_s, 1.0, 0.0)

    def order(key_l, key_s):
        tie = jnp.where(key_l == key_s, jnp.where(lane < sub, live_l, 0.0), 0.0)
        rank = jnp.sum(jnp.where(key_l < key_s, live_l, tie), axis=1, keepdims=True)
        hit = jnp.where(rank == lane_f, live_s, 0.0)
        return jnp.sum(hit * sub_f, axis=0, keepdims=True)

    col_l, col_s = spread(cols_ref[...])
    row_l, row_s = spread(rows_ref[...])
    upto = jnp.sum(jnp.where(col_s <= col_l, live_s, 0.0), axis=0, keepdims=True)
    last = jnp.where(live_l[0:1] > 0.5, upto - 1.0, float(DEAD))
    number = jnp.sum(live_s, axis=0, keepdims=True)
    for at, row in (
        (BY_COL, order(col_l, col_s)), (BY_ROW, order(row_l, row_s)), (LAST, last), (LIVE, number)
    ):
        tab_ref[at:at + 1, :] = row.astype(jnp.int32)


def gather_kernel(
    rows_hbm, cols_hbm, counts_hbm, up_ref, dn_ref, x_hbm, dy_hbm,
    gu_ref, gd_ref, x_ref, dy_ref, tab_ref, rows_ref, cols_ref, counts,
    own_sem, send_sem, recv_sem,
):
    spot = Spot()
    mine = (up_ref, dn_ref)
    full = (gu_ref, gd_ref)
    first_p, first_m = {"fsdp": spot.owner(1, 0)}, {"fsdp": spot.owner(3, 0)}
    second_p, second_m = {"fsdp": spot.owner(0, 1)}, {"fsdp": spot.owner(0, 3)}
    other = {"fsdp": spot.sibling()}
    mail = Mail(send_sem, recv_sem)
    me = spot.owner(0, 0)

    def held(i, j, h):
        return mine[h] if (i, j) == (0, 0) else full[h].at[spot.owner(i, j)]

    def place(i, j, h):
        return full[h].at[spot.owner(i, j)]

    def arrive(i, j, h, key, source):
        mail.wait(place(i, j, h), key, source)

    def share(i, j, h):
        mail.send(held(i, j, h), place(i, j, h), other, h, lane=1)

    def second(i, h):
        mail.send(held(i, 0, h), place(i, 0, h), second_p, ("sec", i, 3, h))
        mail.send(held(i, 0, h), place(i, 0, h), second_m, ("sec", i, 1, h))

    keeps = [
        pltpu.make_async_copy(src, dst, own_sem.at[n])
        for n, (src, dst) in enumerate((
            (up_ref, gu_ref.at[me]), (dn_ref, gd_ref.at[me]),
            (x_ref, x_ref), (dy_ref, dy_ref),
            (rows_hbm, rows_ref), (cols_hbm, cols_ref), (counts_hbm, counts),
        ))
    ]
    blocks = x_ref.shape[0]

    def cut(b, carry):
        at = pl.ds(pl.multiple_of(b * EDGE, EDGE), EDGE)
        pltpu.make_async_copy(x_hbm.at[:, at], x_ref.at[b], own_sem.at[2]).start()
        pltpu.make_async_copy(dy_hbm.at[:, at], dy_ref.at[b], own_sem.at[3]).start()
        return carry

    def load():
        for n in (4, 5, 6, 0, 1):
            keeps[n].start()
        lax.fori_loop(0, blocks, cut, 0)

    greet([first_p, first_m, second_p, second_m, other], load)
    for h in (0, 1):
        mail.send(mine[h], place(0, 0, h), first_p, ("fst", 3, h))
        mail.send(mine[1 - h], place(0, 0, 1 - h), first_m, ("fst", 1, 1 - h))
    for h in (0, 1):
        second(0, h)
    for h in (0, 1):
        share(0, 0, h)
    for n in (4, 5, 6):
        keeps[n].wait()
    slot_tables(rows_ref, cols_ref, counts, tab_ref)
    arrive(3, 0, 0, ("fst", 3, 0), first_m)
    mail.send(held(3, 0, 0), place(3, 0, 0), first_p, ("fst", 2, 0))
    arrive(1, 0, 1, ("fst", 1, 1), first_p)
    mail.send(held(1, 0, 1), place(1, 0, 1), first_m, ("fst", 2, 1))
    second(3, 0)
    second(1, 1)
    share(3, 0, 0)
    share(1, 0, 1)
    arrive(3, 0, 1, ("fst", 3, 1), first_m)
    second(3, 1)
    share(3, 0, 1)
    arrive(1, 0, 0, ("fst", 1, 0), first_p)
    second(1, 0)
    share(1, 0, 0)
    arrive(2, 0, 0, ("fst", 2, 0), first_m)
    second(2, 0)
    share(2, 0, 0)
    arrive(2, 0, 1, ("fst", 2, 1), first_p)
    second(2, 1)
    share(2, 0, 1)
    for i in (0, 3, 1, 2):
        arrive(i, 3, 0, ("sec", i, 3, 0), second_m)
        mail.send(held(i, 3, 0), place(i, 3, 0), second_p, ("sec", i, 2, 0))
        share(i, 3, 0)
        arrive(i, 1, 1, ("sec", i, 1, 1), second_p)
        mail.send(held(i, 1, 1), place(i, 1, 1), second_m, ("sec", i, 2, 1))
        share(i, 1, 1)
        arrive(i, 3, 1, ("sec", i, 3, 1), second_m)
        share(i, 3, 1)
        arrive(i, 1, 0, ("sec", i, 1, 0), second_p)
        share(i, 1, 0)
    for i in (0, 3, 1, 2):
        arrive(i, 2, 0, ("sec", i, 2, 0), second_m)
        share(i, 2, 0)
        arrive(i, 2, 1, ("sec", i, 2, 1), second_p)
        share(i, 2, 1)
    for h in (0, 1):
        mail.wait(full[h].at[pl.ds(0, RING * RING)], h, other)
    for n in range(4):
        keeps[n].wait()
    mail.sent_all(gu_ref.at[pl.ds(0, RING_COPIES)], other, 0)
    mail.sent_all(gu_ref, other, 1)
    assert len(mail.keys) == RING_COPIES and mail.sent == RING_COPIES + gu_ref.shape[0]


def gather_weights(rows, cols, counts, up, dn, x, dy):
    owners = 2 * RING * RING
    any_spec = pl.BlockSpec(memory_space=pltpu.HBM)
    vmem_spec = pl.BlockSpec(memory_space=pltpu.VMEM)
    full = pltpu.VMEM((owners,) + up.shape, up.dtype)
    cut = pltpu.VMEM((x.shape[1] // EDGE, x.shape[0], EDGE), x.dtype)
    return pl.pallas_call(
        gather_kernel,
        out_shape=(
            full, full, cut, cut,
            jax.ShapeDtypeStruct((8, SLOT_TOTAL), jnp.int32),
        ),
        in_specs=[any_spec] * 7,
        out_specs=(vmem_spec,) * 5,
        scratch_shapes=[
            pltpu.VMEM((1, SLOT_TOTAL), jnp.int32),
            pltpu.VMEM((1, SLOT_TOTAL), jnp.int32),
            pltpu.SMEM(counts.shape, jnp.int32),
            pltpu.SemaphoreType.DMA((7,)),
            pltpu.SemaphoreType.DMA((2,)),
            pltpu.SemaphoreType.DMA((2 + RING_COPIES,)),
        ],
        compiler_params=pltpu.CompilerParams(
            collective_id=0, has_side_effects=True, vmem_limit_bytes=VM_K1
        ),
        name="gather_weights",
    )(
        in_hbm(rows.reshape(1, SLOT_TOTAL)), in_hbm(cols.reshape(1, SLOT_TOTAL)), in_hbm(counts),
        in_hbm(up), in_hbm(dn), in_hbm(x), in_hbm(dy),
    )


NT = (((1,), (1,)), ((), ()))
TN = (((0,), (0,)), ((), ()))
NN = (((1,), (0,)), ((), ()))


def mm(a, b, dims):
    return lax.dot_general(a, b, dims, preferred_element_type=F32)


UNROLL, REST = 10, 2


def layer_kernel(
    rows, cols, tab, x, dy, up, dn, out_hbm, in_hbm, hid, pgr, out, inp, acc, sem
):
    row_blocks, tok = x.shape[:2]
    width = row_blocks * EDGE
    n_live = tab[LIVE, 0]
    whole = n_live // UNROLL
    rest = (n_live - whole * UNROLL + REST - 1) // REST

    def block(b):
        return pl.ds(pl.multiple_of(b * EDGE, EDGE), EDGE)

    hid[DEAD] = jnp.zeros((tok, EDGE), BF16)
    pgr[DEAD] = jnp.zeros((tok, EDGE), BF16)

    def forward(width, start, step, carry):
        pre, back = acc[0], acc[1]
        for u in range(width):
            s = start + step * width + u
            k = tab[BY_COL, jnp.minimum(s, n_live - 1)]
            before = tab[BY_COL, jnp.clip(s - 1, 0, n_live - 1)]
            r = rows[k]
            first = jnp.logical_or(s == 0, cols[before] != cols[k])
            pre = jnp.where(first, 0.0, pre) + mm(x[r], up[k], NN)
            back = jnp.where(first, 0.0, back) + mm(dy[r], dn[k], NT)
            value, slope = gelu_parts(pre)
            to = jnp.where(s < n_live, s, DEAD + 1)
            hid[to] = value.astype(BF16)
            pgr[to] = (back * slope).astype(BF16)
        acc[0] = pre
        acc[1] = back
        return carry

    lax.fori_loop(0, whole, functools.partial(forward, UNROLL, 0), 0)
    lax.fori_loop(0, rest, functools.partial(forward, REST, whole * UNROLL), 0)

    def clear(b, carry):
        out[:, block(b)] = jnp.zeros((tok, EDGE), BF16)
        inp[:, block(b)] = jnp.zeros((tok, EDGE), BF16)
        return carry

    lax.fori_loop(0, row_blocks, clear, 0)

    def put(b, carry):
        pltpu.make_async_copy(out.at[:, block(b)], out_hbm.at[:, block(b)], sem.at[0]).start()
        pltpu.make_async_copy(inp.at[:, block(b)], in_hbm.at[:, block(b)], sem.at[1]).start()
        return carry

    def backward(width, start, step, done):
        o, g = acc[0], acc[1]
        for u in range(width):
            t = start + step * width + u
            k = tab[BY_ROW, jnp.minimum(t, n_live - 1)]
            r = rows[k]
            before = tab[BY_ROW, jnp.clip(t - 1, 0, n_live - 1)]
            to = block(jnp.where(t < n_live, r, row_blocks))
            first = jnp.logical_or(t == 0, rows[before] != r)
            last = tab[LAST, k]
            o = jnp.where(first, 0.0, o) + mm(hid[last], dn[k], NN)
            g = jnp.where(first, 0.0, g) + mm(pgr[last], up[k], NT)
            out[:, to] = o.astype(BF16)
            inp[:, to] = g.astype(BF16)
        acc[0] = o
        acc[1] = g
        upto = rows[tab[BY_ROW, jnp.minimum(start + (step + 1) * width - 1, n_live - 1)]]
        lax.fori_loop(done, upto, put, 0)
        return upto

    done = lax.fori_loop(0, whole, functools.partial(backward, UNROLL, 0), 0)
    done = lax.fori_loop(0, rest, functools.partial(backward, REST, whole * UNROLL), done)
    lax.fori_loop(done, row_blocks, put, 0)
    every = pl.ds(0, width)
    pltpu.make_async_copy(out.at[:, every], out_hbm, sem.at[0]).wait()
    pltpu.make_async_copy(inp.at[:, every], in_hbm, sem.at[1]).wait()


def local_layer(rows, cols, tab, x, dy, up, dn):
    row_blocks, tok = x.shape[:2]
    width = row_blocks * EDGE
    any_spec = pl.BlockSpec(memory_space=pl.ANY)
    smem_spec = pl.BlockSpec(memory_space=pltpu.SMEM)
    vmem_spec = pl.BlockSpec(memory_space=pltpu.VMEM)
    kept = pltpu.VMEM((SLOT_TOTAL + 2, tok, EDGE), BF16)
    result = jax.ShapeDtypeStruct((tok, width), BF16)
    return pl.pallas_call(
        layer_kernel,
        out_shape=(result, result, kept, kept),
        in_specs=[smem_spec] * 3 + [vmem_spec] * 4,
        out_specs=(any_spec,) * 2 + (vmem_spec,) * 2,
        scratch_shapes=[
            pltpu.VMEM((tok, width + EDGE), BF16),
            pltpu.VMEM((tok, width + EDGE), BF16),
            pltpu.VMEM((2, tok, EDGE), F32),
            pltpu.SemaphoreType.DMA((2,)),
        ],
        compiler_params=pltpu.CompilerParams(vmem_limit_bytes=VM_K2),
        name="local_layer",
    )(
        rows, cols, tab, in_vmem(x), in_vmem(dy),
        in_vmem(up.reshape(SLOT_TOTAL, EDGE, EDGE)), in_vmem(dn.reshape(SLOT_TOTAL, EDGE, EDGE)),
    )


VM_K2 = 16 << 20


def in_hbm(array):
    return pltpu.with_memory_space_constraint(array, pltpu.HBM)


def in_vmem(array):
    return pltpu.with_memory_space_constraint(array, pltpu.VMEM)


TAIL = 4
RS_COPIES = 40 + 10 * TAIL
VM_K3 = 26 << 20


def scatter_kernel(
    scale, rows, tab, x, dy, hid, pgr, ug_ref, dg_ref,
    stage, own, sib, mid, got_m, got_p, r_own, r_bf, r_f32, mid2, fin_m, fin_p, zsend, zrecv,
    send_sem, recv_sem,
):
    spot = Spot()
    final = (ug_ref, dg_ref)
    first_p, first_m = {"fsdp": spot.owner(1, 0)}, {"fsdp": spot.owner(3, 0)}
    second_p, second_m = {"fsdp": spot.owner(0, 1)}, {"fsdp": spot.owner(0, 3)}
    other = {"fsdp": spot.sibling()}
    z_a = {"dp": spot.z + 1 - 2 * lax.rem(spot.z, 2)}
    z_b = {"dp": RING - 1 - spot.z}
    mail = Mail(send_sem, recv_sem)

    def partial(owner, h, q):
        k = owner * SLOTS + q
        if h == 0:
            return mm(x[rows[k]], pgr[tab[LAST, k]], TN)
        return mm(hid[tab[LAST, k]], dy[rows[k]], TN)

    def make(i, j):
        at = i * RING + j
        for h in (0, 1):
            for q in range(SLOTS):
                stage[at, h, q] = partial(spot.owner(i, j, 1 - spot.c), h, q).astype(BF16)

    def give(i, j):
        at = i * RING + j
        mail.send_at(stage.at[at], sib.at[at], other, at, 0)

    def given(i, j):
        at = i * RING + j
        mail.wait_at(sib.at[at], other, at)

    def keep(i, j, h, *more):
        at = i * RING + j
        for q in range(SLOTS):
            value = partial(spot.owner(i, j), h, q) + sib[at, h, q].astype(F32)
            for ref in more:
                value = value + ref[q].astype(F32)
            own[at, h, q] = value.astype(BF16)
        return own.at[at, h]

    shares = [pl.ds(p * SLOTS // TAIL, SLOTS // TAIL) for p in range(TAIL)]
    mids = RING * RING
    base = mids + 2 * RING
    one = base + 4 * RING

    def turns(*acts):
        def step(n, carry):
            for act in acts:
                act(turn(n))
            return carry
        return step

    def make_give(j):
        def act(i):
            make(i, j)
            give(i, j)
        return act

    def far(i):
        given(i, 2)
        mail.send_at(keep(i, 2, 0), mid.at[i, 0], second_p, mids + i, 1)
        mail.send_at(keep(i, 2, 1), mid.at[i, 1], second_m, mids + RING + i, 1)

    def near(i):
        given(i, 1)
        mail.send_at(keep(i, 1, 1), got_m.at[i, 1], second_p, base + i, 1)
        given(i, 3)
        mail.send_at(keep(i, 3, 0), got_p.at[i, 0], second_m, base + RING + i, 1)
        mail.wait_at(mid.at[i, 0], second_m, mids + i)
        mail.send_at(keep(i, 1, 0, mid.at[i, 0]), got_m.at[i, 0], second_p, base + 2 * RING + i, 1)
        mail.wait_at(mid.at[i, 1], second_p, mids + RING + i)
        mail.send_at(keep(i, 3, 1, mid.at[i, 1]), got_p.at[i, 1], second_m, base + 3 * RING + i, 1)

    def stay(i):
        given(i, 0)
        at = i * RING
        for h in (0, 1):
            for q in range(SLOTS):
                r_own[i, h, q] = partial(spot.owner(i, 0), h, q) + sib[at, h, q].astype(F32)

    def rung(i, h):
        mail.wait_at(got_m.at[i, h], second_m, base + (2 * RING, 0)[h] + i)
        mail.wait_at(got_p.at[i, h], second_p, base + (RING, 3 * RING)[h] + i)

    def ring_sum(i, h, of):
        return r_own[i, h, of] + got_m[i, h, of].astype(F32) + got_p[i, h, of].astype(F32)

    def pass_on(n, i, h, dst, target):
        rung(i, h)
        for p, of in enumerate(shares):
            r_bf[n, of] = ring_sum(i, h, of).astype(BF16)
            mail.send_at(r_bf.at[n, of], dst.at[h, of], target, one + 6 * p + n, 2)

    def add_on(p, of, n, i, h, dst, target):
        value = ring_sum(i, h, of)
        mail.wait_at(mid2.at[h, of], (first_m, first_p)[h], one + 6 * p + h)
        r_bf[4 + n, of] = (value + mid2[h, of].astype(F32)).astype(BF16)
        mail.send_at(r_bf.at[4 + n, of], dst.at[h, of], target, one + 6 * p + 4 + n, 2)

    greet(
        [first_p, first_m, second_p, second_m, other, z_a, z_b],
        lambda: lax.fori_loop(0, RING, turns(lambda i: make(i, 2)), 0),
    )
    lax.fori_loop(0, 4, turns(lambda i: give(i, 2)), 0)
    lax.fori_loop(0, 4, turns(far, make_give(3), make_give(1)), 0)
    lax.fori_loop(0, 4, turns(near, make_give(0)), 0)
    lax.fori_loop(0, 4, turns(stay), 0)
    pass_on(0, 2, 0, mid2, first_p)
    pass_on(1, 2, 1, mid2, first_m)
    pass_on(2, 1, 1, fin_m, first_p)
    pass_on(3, 3, 0, fin_p, first_m)
    rung(1, 0)
    rung(3, 1)
    for p, of in enumerate(shares):
        add_on(p, of, 0, 1, 0, fin_m, first_p)
        add_on(p, of, 1, 3, 1, fin_p, first_m)
    for h in (0, 1):
        rung(0, h)
        r_f32[h] = ring_sum(0, h, slice(None))
    plane = one + 6 * TAIL
    for p, of in enumerate(shares):
        for h in (0, 1):
            mail.wait_at(fin_m.at[h, of], first_m, one + 6 * p + (4, 2)[h])
            mail.wait_at(fin_p.at[h, of], first_p, one + 6 * p + (3, 5)[h])
            value = r_f32[h, of] + fin_m[h, of].astype(F32) + fin_p[h, of].astype(F32)
            zsend[0, h, of] = value.astype(BF16)
            mail.send_at(
                zsend.at[0, h, of], zrecv.at[0, h, of], (z_a, z_b)[h], plane + 4 * p + h, 2
            )
    for p, of in enumerate(shares):
        for h in (0, 1):
            mail.wait_at(zrecv.at[0, h, of], (z_a, z_b)[h], plane + 4 * p + h)
            value = zsend[0, h, of].astype(F32) + zrecv[0, h, of].astype(F32)
            zsend[1, h, of] = value.astype(BF16)
            mail.send_at(
                zsend.at[1, h, of], zrecv.at[1, h, of], (z_b, z_a)[h], plane + 4 * p + 2 + h, 2
            )
    for p, of in enumerate(shares):
        for h in (0, 1):
            mail.wait_at(zrecv.at[1, h, of], (z_b, z_a)[h], plane + 4 * p + 2 + h)
            value = zsend[1, h, of].astype(F32) + zrecv[1, h, of].astype(F32)
            final[h][of] = value * scale

    mail.sent_all(stage, other, 0)
    mail.sent_all(own.at[pl.ds(0, 3 * RING)], other, 1)
    mail.sent_all(own.at[pl.ds(0, 5)], other, 2)


def turn(n):
    return lax.rem(2 + n * (n + 1) // 2, RING)


def scatter_grads(rows, tab, x, dy, hid, pgr, scale):
    piece = (SLOTS, EDGE, EDGE)
    grad = jax.ShapeDtypeStruct(piece, F32)
    vmem = pl.BlockSpec(memory_space=pltpu.VMEM)
    smem = pl.BlockSpec(memory_space=pltpu.SMEM)
    return pl.pallas_call(
        functools.partial(scatter_kernel, scale),
        out_shape=(grad, grad),
        in_specs=[smem] * 2 + [vmem] * 4,
        out_specs=(vmem, vmem),
        scratch_shapes=[
            pltpu.VMEM((RING * RING, 2) + piece, BF16),
            pltpu.VMEM((RING * RING, 2) + piece, BF16),
            pltpu.VMEM((RING * RING, 2) + piece, BF16),
            pltpu.VMEM((RING, 2) + piece, BF16),
            pltpu.VMEM((RING, 2) + piece, BF16),
            pltpu.VMEM((RING, 2) + piece, BF16),
            pltpu.VMEM((RING, 2) + piece, F32),
            pltpu.VMEM((6,) + piece, BF16),
            pltpu.VMEM((2,) + piece, F32),
            pltpu.VMEM((2,) + piece, BF16),
            pltpu.VMEM((2,) + piece, BF16),
            pltpu.VMEM((2,) + piece, BF16),
            pltpu.VMEM((2, 2) + piece, BF16),
            pltpu.VMEM((2, 2) + piece, BF16),
            pltpu.SemaphoreType.DMA((3,)),
            pltpu.SemaphoreType.DMA((RS_COPIES,)),
        ],
        compiler_params=pltpu.CompilerParams(
            collective_id=1, has_side_effects=True, vmem_limit_bytes=VM_K3
        ),
        name="scatter_grads",
    )(rows, tab, in_vmem(x), in_vmem(dy), in_vmem(hid), in_vmem(pgr))


def on_device(tokens, cotangent, up_w, dn_w, block_rows, block_cols, owner_counts):
    devices = lax.axis_size("dp") * lax.axis_size("fsdp")
    scale = 1.0 / math.sqrt(tokens.shape[0] * devices)
    up_full, dn_full, x, dy, tab = gather_weights(
        block_rows, block_cols, owner_counts, up_w, dn_w, tokens, cotangent
    )
    output, input_grad, hid, pgr = local_layer(
        block_rows, block_cols, tab, x, dy, up_full, dn_full
    )
    up_grad, down_grad = scatter_grads(block_rows, tab, x, dy, hid, pgr, scale)
    return output, input_grad, up_grad, down_grad


def solution(mesh):
    in_specs = (
        P(("dp", "fsdp"), None),
        P(("dp", "fsdp"), None),
        P("fsdp", None, None),
        P("fsdp", None, None),
        P(),
        P(),
        P(),
    )
    out_specs = (
        P(("dp", "fsdp"), None),
        P(("dp", "fsdp"), None),
        P("fsdp", None, None),
        P("fsdp", None, None),
    )
    return jax.shard_map(
        on_device, mesh=mesh, in_specs=in_specs, out_specs=out_specs, check_vma=False
    )
```

```python
import functools
import math

import jax
import jax.numpy as jnp
from jax import lax
from jax.experimental import pallas as pl
from jax.experimental.pallas import tpu as pltpu
from jax.sharding import PartitionSpec as P

EDGE = 128
SLOTS = 4
RING = 4
MESH_ID = pl.DeviceIdType.MESH
BF16 = jnp.bfloat16
F32 = jnp.float32

gelu_scale = 0.7978845608028654
cubic_coef = 0.044715


def gelu_parts(values):
    square = values * values
    tanh_val = jnp.tanh(values * (gelu_scale + gelu_scale * cubic_coef * square))
    half = 0.5 * values
    above, below = 1.0 + tanh_val, 1.0 - tanh_val
    gelu_value = half * above
    gelu_slope = above * (
        0.5 + half * below * (gelu_scale + 3.0 * gelu_scale * cubic_coef * square)
    )
    return gelu_value, gelu_slope


class Spot:
    def __init__(self):
        me = lax.axis_index("fsdp")
        self.z = lax.axis_index("dp")
        self.c = lax.rem(me, 2)
        self.y = lax.rem(me // 2, RING)
        self.x = me // (2 * RING)

    def owner(self, i, j, c=None):
        c = self.c if c is None else c
        x = lax.rem(self.x + i * (1 - c) + j * c, RING)
        y = lax.rem(self.y + i * c + j * (1 - c), RING)
        return (x * RING + y) * 2 + c

    def sibling(self):
        return (self.x * RING + self.y) * 2 + (1 - self.c)


def greet(targets, meanwhile=None):
    barrier = pltpu.get_barrier_semaphore()
    for target in targets:
        pl.semaphore_signal(barrier, inc=1, device_id=target, device_id_type=MESH_ID)
    if meanwhile is not None:
        meanwhile()
    pl.semaphore_wait(barrier, len(targets))


class Mail:
    def __init__(self, send_sem, recv_sem):
        self.send_sem, self.recv_sem = send_sem, recv_sem
        self.keys, self.sent = {}, 0

    def copy(self, src, dst, target, n, lane):
        return pltpu.make_async_remote_copy(
            src_ref=src,
            dst_ref=dst,
            send_sem=self.send_sem.at[lane],
            recv_sem=self.recv_sem.at[n],
            device_id=target,
            device_id_type=MESH_ID,
        )

    def slot(self, key):
        return key if isinstance(key, int) else self.keys.setdefault(key, 2 + len(self.keys))

    def send(self, src, dst, target, key, lane=0):
        self.copy(src, dst, target, self.slot(key), lane).start()
        self.sent += 1

    def wait(self, dst, key, target):
        self.copy(dst, dst, target, self.slot(key), 0).wait_recv()

    def send_at(self, src, dst, target, n, lane):
        self.copy(src, dst, target, n, lane).start()

    def wait_at(self, dst, target, n):
        self.copy(dst, dst, target, n, 0).wait_recv()

    def sent_all(self, like, target, lane):
        self.copy(like, like, target, 0, lane).wait_send()


VM_K1 = 8 << 20
RING_COPIES = 30
SLOT_TOTAL = 128
DEAD = SLOT_TOTAL
BY_COL, BY_ROW, LAST, LIVE = 0, 1, 2, 3


def slot_tables(rows_ref, cols_ref, counts, tab_ref):
    n = SLOT_TOTAL
    lane = lax.broadcasted_iota(jnp.int32, (n, n), 1)
    sub = lax.broadcasted_iota(jnp.int32, (n, n), 0)
    lane_owner = lax.broadcasted_iota(jnp.int32, (8, n), 1) // SLOTS
    held = jnp.zeros((8, n), jnp.int32)
    for o in range(n // SLOTS):
        held = jnp.where(lane_owner == o, counts[o], held)
    lane_f, sub_f = lane.astype(F32), sub.astype(F32)

    def spread(row):
        across = jnp.broadcast_to(row.astype(F32), (n, n))
        return across, across.T

    held_l, held_s = spread(held[0:1])
    slot_l = lax.rem(lane, SLOTS).astype(F32)
    slot_s = lax.rem(sub, SLOTS).astype(F32)
    live_l = jnp.where(slot_l < held_l, 1.0, 0.0)
    live_s = jnp.where(slot_s < held_s, 1.0, 0.0)

    def order(key_l, key_s):
        tie = jnp.where(key_l == key_s, jnp.where(lane < sub, live_l, 0.0), 0.0)
        rank = jnp.sum(jnp.where(key_l < key_s, live_l, tie), axis=1, keepdims=True)
        hit = jnp.where(rank == lane_f, live_s, 0.0)
        return jnp.sum(hit * sub_f, axis=0, keepdims=True)

    col_l, col_s = spread(cols_ref[...])
    row_l, row_s = spread(rows_ref[...])
    upto = jnp.sum(jnp.where(col_s <= col_l, live_s, 0.0), axis=0, keepdims=True)
    last = jnp.where(live_l[0:1] > 0.5, upto - 1.0, float(DEAD))
    number = jnp.sum(live_s, axis=0, keepdims=True)
    for at, row in (
        (BY_COL, order(col_l, col_s)), (BY_ROW, order(row_l, row_s)), (LAST, last), (LIVE, number)
    ):
        tab_ref[at:at + 1, :] = row.astype(jnp.int32)


def gather_kernel(
    rows_hbm, cols_hbm, counts_hbm, up_ref, dn_ref, x_hbm, dy_hbm,
    gu_ref, gd_ref, x_ref, dy_ref, tab_ref, rows_ref, cols_ref, counts,
    own_sem, send_sem, recv_sem,
):
    spot = Spot()
    mine = (up_ref, dn_ref)
    full = (gu_ref, gd_ref)
    first_p, first_m = {"fsdp": spot.owner(1, 0)}, {"fsdp": spot.owner(3, 0)}
    second_p, second_m = {"fsdp": spot.owner(0, 1)}, {"fsdp": spot.owner(0, 3)}
    other = {"fsdp": spot.sibling()}
    mail = Mail(send_sem, recv_sem)
    me = spot.owner(0, 0)

    def held(i, j, h):
        return mine[h] if (i, j) == (0, 0) else full[h].at[spot.owner(i, j)]

    def place(i, j, h):
        return full[h].at[spot.owner(i, j)]

    def arrive(i, j, h, key, source):
        mail.wait(place(i, j, h), key, source)

    def share(i, j, h):
        mail.send(held(i, j, h), place(i, j, h), other, h, lane=1)

    def second(i, h):
        mail.send(held(i, 0, h), place(i, 0, h), second_p, ("sec", i, 3, h))
        mail.send(held(i, 0, h), place(i, 0, h), second_m, ("sec", i, 1, h))

    keeps = [
        pltpu.make_async_copy(src, dst, own_sem.at[n])
        for n, (src, dst) in enumerate((
            (up_ref, gu_ref.at[me]), (dn_ref, gd_ref.at[me]),
            (x_ref, x_ref), (dy_ref, dy_ref),
            (rows_hbm, rows_ref), (cols_hbm, cols_ref), (counts_hbm, counts),
        ))
    ]
    blocks = x_ref.shape[0]

    def cut(b, carry):
        at = pl.ds(pl.multiple_of(b * EDGE, EDGE), EDGE)
        pltpu.make_async_copy(x_hbm.at[:, at], x_ref.at[b], own_sem.at[2]).start()
        pltpu.make_async_copy(dy_hbm.at[:, at], dy_ref.at[b], own_sem.at[3]).start()
        return carry

    def load():
        for n in (4, 5, 6, 0, 1):
            keeps[n].start()
        lax.fori_loop(0, blocks, cut, 0)

    greet([first_p, first_m, second_p, second_m, other], load)
    for h in (0, 1):
        mail.send(mine[h], place(0, 0, h), first_p, ("fst", 3, h))
        mail.send(mine[1 - h], place(0, 0, 1 - h), first_m, ("fst", 1, 1 - h))
    for h in (0, 1):
        second(0, h)
    for h in (0, 1):
        share(0, 0, h)
    for n in (4, 5, 6):
        keeps[n].wait()
    slot_tables(rows_ref, cols_ref, counts, tab_ref)
    arrive(3, 0, 0, ("fst", 3, 0), first_m)
    mail.send(held(3, 0, 0), place(3, 0, 0), first_p, ("fst", 2, 0))
    arrive(1, 0, 1, ("fst", 1, 1), first_p)
    mail.send(held(1, 0, 1), place(1, 0, 1), first_m, ("fst", 2, 1))
    second(3, 0)
    second(1, 1)
    share(3, 0, 0)
    share(1, 0, 1)
    arrive(3, 0, 1, ("fst", 3, 1), first_m)
    second(3, 1)
    share(3, 0, 1)
    arrive(1, 0, 0, ("fst", 1, 0), first_p)
    second(1, 0)
    share(1, 0, 0)
    arrive(2, 0, 0, ("fst", 2, 0), first_m)
    second(2, 0)
    share(2, 0, 0)
    arrive(2, 0, 1, ("fst", 2, 1), first_p)
    second(2, 1)
    share(2, 0, 1)
    for i in (0, 3, 1, 2):
        arrive(i, 3, 0, ("sec", i, 3, 0), second_m)
        mail.send(held(i, 3, 0), place(i, 3, 0), second_p, ("sec", i, 2, 0))
        share(i, 3, 0)
        arrive(i, 1, 1, ("sec", i, 1, 1), second_p)
        mail.send(held(i, 1, 1), place(i, 1, 1), second_m, ("sec", i, 2, 1))
        share(i, 1, 1)
        arrive(i, 3, 1, ("sec", i, 3, 1), second_m)
        share(i, 3, 1)
        arrive(i, 1, 0, ("sec", i, 1, 0), second_p)
        share(i, 1, 0)
    for i in (0, 3, 1, 2):
        arrive(i, 2, 0, ("sec", i, 2, 0), second_m)
        share(i, 2, 0)
        arrive(i, 2, 1, ("sec", i, 2, 1), second_p)
        share(i, 2, 1)
    for h in (0, 1):
        mail.wait(full[h].at[pl.ds(0, RING * RING)], h, other)
    for n in range(4):
        keeps[n].wait()
    mail.sent_all(gu_ref.at[pl.ds(0, RING_COPIES)], other, 0)
    mail.sent_all(gu_ref, other, 1)
    assert len(mail.keys) == RING_COPIES and mail.sent == RING_COPIES + gu_ref.shape[0]


def gather_weights(rows, cols, counts, up, dn, x, dy):
    owners = 2 * RING * RING
    any_spec = pl.BlockSpec(memory_space=pltpu.HBM)
    vmem_spec = pl.BlockSpec(memory_space=pltpu.VMEM)
    full = pltpu.VMEM((owners,) + up.shape, up.dtype)
    cut = pltpu.VMEM((x.shape[1] // EDGE, x.shape[0], EDGE), x.dtype)
    return pl.pallas_call(
        gather_kernel,
        out_shape=(
            full, full, cut, cut,
            jax.ShapeDtypeStruct((8, SLOT_TOTAL), jnp.int32),
        ),
        in_specs=[any_spec] * 7,
        out_specs=(vmem_spec,) * 5,
        scratch_shapes=[
            pltpu.VMEM((1, SLOT_TOTAL), jnp.int32),
            pltpu.VMEM((1, SLOT_TOTAL), jnp.int32),
            pltpu.SMEM(counts.shape, jnp.int32),
            pltpu.SemaphoreType.DMA((7,)),
            pltpu.SemaphoreType.DMA((2,)),
            pltpu.SemaphoreType.DMA((2 + RING_COPIES,)),
        ],
        compiler_params=pltpu.CompilerParams(
            collective_id=0, has_side_effects=True, vmem_limit_bytes=VM_K1
        ),
        name="gather_weights",
    )(
        in_hbm(rows.reshape(1, SLOT_TOTAL)), in_hbm(cols.reshape(1, SLOT_TOTAL)), in_hbm(counts),
        in_hbm(up), in_hbm(dn), in_hbm(x), in_hbm(dy),
    )


NT = (((1,), (1,)), ((), ()))
TN = (((0,), (0,)), ((), ()))
NN = (((1,), (0,)), ((), ()))


def mm(a, b, dims):
    return lax.dot_general(a, b, dims, preferred_element_type=F32)


UNROLL, REST = 10, 2


def layer_kernel(
    rows, cols, tab, x, dy, up, dn, out_hbm, in_hbm, hid, pgr, out, inp, acc, sem
):
    row_blocks, tok = x.shape[:2]
    width = row_blocks * EDGE
    n_live = tab[LIVE, 0]
    whole = n_live // UNROLL
    rest = (n_live - whole * UNROLL + REST - 1) // REST

    def block(b):
        return pl.ds(pl.multiple_of(b * EDGE, EDGE), EDGE)

    hid[DEAD] = jnp.zeros((tok, EDGE), BF16)
    pgr[DEAD] = jnp.zeros((tok, EDGE), BF16)

    def forward(width, start, step, carry):
        pre, back = acc[0], acc[1]
        for u in range(width):
            s = start + step * width + u
            k = tab[BY_COL, jnp.minimum(s, n_live - 1)]
            before = tab[BY_COL, jnp.clip(s - 1, 0, n_live - 1)]
            r = rows[k]
            first = jnp.logical_or(s == 0, cols[before] != cols[k])
            pre = jnp.where(first, 0.0, pre) + mm(x[r], up[k], NN)
            back = jnp.where(first, 0.0, back) + mm(dy[r], dn[k], NT)
            value, slope = gelu_parts(pre)
            to = jnp.where(s < n_live, s, DEAD + 1)
            hid[to] = value.astype(BF16)
            pgr[to] = (back * slope).astype(BF16)
        acc[0] = pre
        acc[1] = back
        return carry

    lax.fori_loop(0, whole, functools.partial(forward, UNROLL, 0), 0)
    lax.fori_loop(0, rest, functools.partial(forward, REST, whole * UNROLL), 0)

    def clear(b, carry):
        out[:, block(b)] = jnp.zeros((tok, EDGE), BF16)
        inp[:, block(b)] = jnp.zeros((tok, EDGE), BF16)
        return carry

    lax.fori_loop(0, row_blocks, clear, 0)

    def put(b, carry):
        pltpu.make_async_copy(out.at[:, block(b)], out_hbm.at[:, block(b)], sem.at[0]).start()
        pltpu.make_async_copy(inp.at[:, block(b)], in_hbm.at[:, block(b)], sem.at[1]).start()
        return carry

    def backward(width, start, step, done):
        o, g = acc[0], acc[1]
        for u in range(width):
            t = start + step * width + u
            k = tab[BY_ROW, jnp.minimum(t, n_live - 1)]
            r = rows[k]
            before = tab[BY_ROW, jnp.clip(t - 1, 0, n_live - 1)]
            to = block(jnp.where(t < n_live, r, row_blocks))
            first = jnp.logical_or(t == 0, rows[before] != r)
            last = tab[LAST, k]
            o = jnp.where(first, 0.0, o) + mm(hid[last], dn[k], NN)
            g = jnp.where(first, 0.0, g) + mm(pgr[last], up[k], NT)
            out[:, to] = o.astype(BF16)
            inp[:, to] = g.astype(BF16)
        acc[0] = o
        acc[1] = g
        upto = rows[tab[BY_ROW, jnp.minimum(start + (step + 1) * width - 1, n_live - 1)]]
        lax.fori_loop(done, upto, put, 0)
        return upto

    done = lax.fori_loop(0, whole, functools.partial(backward, UNROLL, 0), 0)
    done = lax.fori_loop(0, rest, functools.partial(backward, REST, whole * UNROLL), done)
    lax.fori_loop(done, row_blocks, put, 0)
    every = pl.ds(0, width)
    pltpu.make_async_copy(out.at[:, every], out_hbm, sem.at[0]).wait()
    pltpu.make_async_copy(inp.at[:, every], in_hbm, sem.at[1]).wait()


def local_layer(rows, cols, tab, x, dy, up, dn):
    row_blocks, tok = x.shape[:2]
    width = row_blocks * EDGE
    any_spec = pl.BlockSpec(memory_space=pl.ANY)
    smem_spec = pl.BlockSpec(memory_space=pltpu.SMEM)
    vmem_spec = pl.BlockSpec(memory_space=pltpu.VMEM)
    kept = pltpu.VMEM((SLOT_TOTAL + 2, tok, EDGE), BF16)
    result = jax.ShapeDtypeStruct((tok, width), BF16)
    return pl.pallas_call(
        layer_kernel,
        out_shape=(result, result, kept, kept),
        in_specs=[smem_spec] * 3 + [vmem_spec] * 4,
        out_specs=(any_spec,) * 2 + (vmem_spec,) * 2,
        scratch_shapes=[
            pltpu.VMEM((tok, width + EDGE), BF16),
            pltpu.VMEM((tok, width + EDGE), BF16),
            pltpu.VMEM((2, tok, EDGE), F32),
            pltpu.SemaphoreType.DMA((2,)),
        ],
        compiler_params=pltpu.CompilerParams(vmem_limit_bytes=VM_K2),
        name="local_layer",
    )(
        rows, cols, tab, in_vmem(x), in_vmem(dy),
        in_vmem(up.reshape(SLOT_TOTAL, EDGE, EDGE)), in_vmem(dn.reshape(SLOT_TOTAL, EDGE, EDGE)),
    )


VM_K2 = 16 << 20


def in_hbm(array):
    return pltpu.with_memory_space_constraint(array, pltpu.HBM)


def in_vmem(array):
    return pltpu.with_memory_space_constraint(array, pltpu.VMEM)


TAIL = 4
RS_COPIES = 40 + 10 * TAIL
VM_K3 = 26 << 20


def scatter_kernel(
    scale, rows, tab, x, dy, hid, pgr, ug_ref, dg_ref,
    stage, own, sib, mid, got_m, got_p, r_own, r_bf, r_f32, mid2, fin_m, fin_p, zsend, zrecv,
    send_sem, recv_sem,
):
    spot = Spot()
    final = (ug_ref, dg_ref)
    first_p, first_m = {"fsdp": spot.owner(1, 0)}, {"fsdp": spot.owner(3, 0)}
    second_p, second_m = {"fsdp": spot.owner(0, 1)}, {"fsdp": spot.owner(0, 3)}
    other = {"fsdp": spot.sibling()}
    z_a = {"dp": spot.z + 1 - 2 * lax.rem(spot.z, 2)}
    z_b = {"dp": RING - 1 - spot.z}
    mail = Mail(send_sem, recv_sem)

    def partial(owner, h, q):
        k = owner * SLOTS + q
        if h == 0:
            return mm(x[rows[k]], pgr[tab[LAST, k]], TN)
        return mm(hid[tab[LAST, k]], dy[rows[k]], TN)

    def make(i, j):
        at = i * RING + j
        for h in (0, 1):
            for q in range(SLOTS):
                stage[at, h, q] = partial(spot.owner(i, j, 1 - spot.c), h, q).astype(BF16)

    def give(i, j):
        at = i * RING + j
        mail.send_at(stage.at[at], sib.at[at], other, at, 0)

    def given(i, j):
        at = i * RING + j
        mail.wait_at(sib.at[at], other, at)

    def keep(i, j, h, *more):
        at = i * RING + j
        for q in range(SLOTS):
            value = partial(spot.owner(i, j), h, q) + sib[at, h, q].astype(F32)
            for ref in more:
                value = value + ref[q].astype(F32)
            own[at, h, q] = value.astype(BF16)
        return own.at[at, h]

    shares = [pl.ds(p * SLOTS // TAIL, SLOTS // TAIL) for p in range(TAIL)]
    mids = RING * RING
    base = mids + 2 * RING
    one = base + 4 * RING

    def turns(*acts):
        def step(n, carry):
            for act in acts:
                act(turn(n))
            return carry
        return step

    def make_give(j):
        def act(i):
            make(i, j)
            give(i, j)
        return act

    def far(i):
        given(i, 2)
        mail.send_at(keep(i, 2, 0), mid.at[i, 0], second_p, mids + i, 1)
        mail.send_at(keep(i, 2, 1), mid.at[i, 1], second_m, mids + RING + i, 1)

    def near(i):
        given(i, 1)
        mail.send_at(keep(i, 1, 1), got_m.at[i, 1], second_p, base + i, 1)
        given(i, 3)
        mail.send_at(keep(i, 3, 0), got_p.at[i, 0], second_m, base + RING + i, 1)
        mail.wait_at(mid.at[i, 0], second_m, mids + i)
        mail.send_at(keep(i, 1, 0, mid.at[i, 0]), got_m.at[i, 0], second_p, base + 2 * RING + i, 1)
        mail.wait_at(mid.at[i, 1], second_p, mids + RING + i)
        mail.send_at(keep(i, 3, 1, mid.at[i, 1]), got_p.at[i, 1], second_m, base + 3 * RING + i, 1)

    def stay(i):
        given(i, 0)
        at = i * RING
        for h in (0, 1):
            for q in range(SLOTS):
                r_own[i, h, q] = partial(spot.owner(i, 0), h, q) + sib[at, h, q].astype(F32)

    def rung(i, h):
        mail.wait_at(got_m.at[i, h], second_m, base + (2 * RING, 0)[h] + i)
        mail.wait_at(got_p.at[i, h], second_p, base + (RING, 3 * RING)[h] + i)

    def ring_sum(i, h, of):
        return r_own[i, h, of] + got_m[i, h, of].astype(F32) + got_p[i, h, of].astype(F32)

    def pass_on(n, i, h, dst, target):
        rung(i, h)
        for p, of in enumerate(shares):
            r_bf[n, of] = ring_sum(i, h, of).astype(BF16)
            mail.send_at(r_bf.at[n, of], dst.at[h, of], target, one + 6 * p + n, 2)

    def add_on(p, of, n, i, h, dst, target):
        value = ring_sum(i, h, of)
        mail.wait_at(mid2.at[h, of], (first_m, first_p)[h], one + 6 * p + h)
        r_bf[4 + n, of] = (value + mid2[h, of].astype(F32)).astype(BF16)
        mail.send_at(r_bf.at[4 + n, of], dst.at[h, of], target, one + 6 * p + 4 + n, 2)

    greet(
        [first_p, first_m, second_p, second_m, other, z_a, z_b],
        lambda: lax.fori_loop(0, RING, turns(lambda i: make(i, 2)), 0),
    )
    lax.fori_loop(0, 4, turns(lambda i: give(i, 2)), 0)
    lax.fori_loop(0, 4, turns(far, make_give(3), make_give(1)), 0)
    lax.fori_loop(0, 4, turns(near, make_give(0)), 0)
    lax.fori_loop(0, 4, turns(stay), 0)
    pass_on(0, 2, 0, mid2, first_p)
    pass_on(1, 2, 1, mid2, first_m)
    pass_on(2, 1, 1, fin_m, first_p)
    pass_on(3, 3, 0, fin_p, first_m)
    rung(1, 0)
    rung(3, 1)
    for p, of in enumerate(shares):
        add_on(p, of, 0, 1, 0, fin_m, first_p)
        add_on(p, of, 1, 3, 1, fin_p, first_m)
    for h in (0, 1):
        rung(0, h)
        r_f32[h] = ring_sum(0, h, slice(None))
    plane = one + 6 * TAIL
    for p, of in enumerate(shares):
        for h in (0, 1):
            mail.wait_at(fin_m.at[h, of], first_m, one + 6 * p + (4, 2)[h])
            mail.wait_at(fin_p.at[h, of], first_p, one + 6 * p + (3, 5)[h])
            value = r_f32[h, of] + fin_m[h, of].astype(F32) + fin_p[h, of].astype(F32)
            zsend[0, h, of] = value.astype(BF16)
            mail.send_at(
                zsend.at[0, h, of], zrecv.at[0, h, of], (z_a, z_b)[h], plane + 4 * p + h, 2
            )
    for p, of in enumerate(shares):
        for h in (0, 1):
            mail.wait_at(zrecv.at[0, h, of], (z_a, z_b)[h], plane + 4 * p + h)
            value = zsend[0, h, of].astype(F32) + zrecv[0, h, of].astype(F32)
            zsend[1, h, of] = value.astype(BF16)
            mail.send_at(
                zsend.at[1, h, of], zrecv.at[1, h, of], (z_b, z_a)[h], plane + 4 * p + 2 + h, 2
            )
    for p, of in enumerate(shares):
        for h in (0, 1):
            mail.wait_at(zrecv.at[1, h, of], (z_b, z_a)[h], plane + 4 * p + 2 + h)
            value = zsend[1, h, of].astype(F32) + zrecv[1, h, of].astype(F32)
            final[h][of] = value * scale

    mail.sent_all(stage, other, 0)
    mail.sent_all(own.at[pl.ds(0, 3 * RING)], other, 1)
    mail.sent_all(own.at[pl.ds(0, 5)], other, 2)


def turn(n):
    return lax.rem(2 + n * (n + 1) // 2, RING)


def scatter_grads(rows, tab, x, dy, hid, pgr, scale):
    piece = (SLOTS, EDGE, EDGE)
    grad = jax.ShapeDtypeStruct(piece, F32)
    vmem = pl.BlockSpec(memory_space=pltpu.VMEM)
    smem = pl.BlockSpec(memory_space=pltpu.SMEM)
    return pl.pallas_call(
        functools.partial(scatter_kernel, scale),
        out_shape=(grad, grad),
        in_specs=[smem] * 2 + [vmem] * 4,
        out_specs=(vmem, vmem),
        scratch_shapes=[
            pltpu.VMEM((RING * RING, 2) + piece, BF16),
            pltpu.VMEM((RING * RING, 2) + piece, BF16),
            pltpu.VMEM((RING * RING, 2) + piece, BF16),
            pltpu.VMEM((RING, 2) + piece, BF16),
            pltpu.VMEM((RING, 2) + piece, BF16),
            pltpu.VMEM((RING, 2) + piece, BF16),
            pltpu.VMEM((RING, 2) + piece, F32),
            pltpu.VMEM((6,) + piece, BF16),
            pltpu.VMEM((2,) + piece, F32),
            pltpu.VMEM((2,) + piece, BF16),
            pltpu.VMEM((2,) + piece, BF16),
            pltpu.VMEM((2,) + piece, BF16),
            pltpu.VMEM((2, 2) + piece, BF16),
            pltpu.VMEM((2, 2) + piece, BF16),
            pltpu.SemaphoreType.DMA((3,)),
            pltpu.SemaphoreType.DMA((RS_COPIES,)),
        ],
        compiler_params=pltpu.CompilerParams(
            collective_id=1, has_side_effects=True, vmem_limit_bytes=VM_K3
        ),
        name="scatter_grads",
    )(rows, tab, in_vmem(x), in_vmem(dy), in_vmem(hid), in_vmem(pgr))


def on_device(tokens, cotangent, up_w, dn_w, block_rows, block_cols, owner_counts):
    devices = lax.axis_size("dp") * lax.axis_size("fsdp")
    scale = 1.0 / math.sqrt(tokens.shape[0] * devices)
    up_full, dn_full, x, dy, tab = gather_weights(
        block_rows, block_cols, owner_counts, up_w, dn_w, tokens, cotangent
    )
    output, input_grad, hid, pgr = local_layer(
        block_rows, block_cols, tab, x, dy, up_full, dn_full
    )
    up_grad, down_grad = scatter_grads(block_rows, tab, x, dy, hid, pgr, scale)
    return output, input_grad, up_grad, down_grad


def solution(mesh):
    in_specs = (
        P(("dp", "fsdp"), None),
        P(("dp", "fsdp"), None),
        P("fsdp", None, None),
        P("fsdp", None, None),
        P(),
        P(),
        P(),
    )
    out_specs = (
        P(("dp", "fsdp"), None),
        P(("dp", "fsdp"), None),
        P("fsdp", None, None),
        P("fsdp", None, None),
    )
    return jax.shard_map(
        on_device, mesh=mesh, in_specs=in_specs, out_specs=out_specs, check_vma=False
    )
```

```python
import functools
import math

import jax
import jax.numpy as jnp
from jax import lax
from jax.experimental import pallas as pl
from jax.experimental.pallas import tpu as pltpu
from jax.sharding import PartitionSpec as P

EDGE = 128
SLOTS = 4
RING = 4
MESH_ID = pl.DeviceIdType.MESH
BF16 = jnp.bfloat16
F32 = jnp.float32

gelu_scale = 0.7978845608028654
cubic_coef = 0.044715


def gelu_parts(values):
    square = values * values
    tanh_val = jnp.tanh(values * (gelu_scale + gelu_scale * cubic_coef * square))
    half = 0.5 * values
    above, below = 1.0 + tanh_val, 1.0 - tanh_val
    gelu_value = half * above
    gelu_slope = above * (
        0.5 + half * below * (gelu_scale + 3.0 * gelu_scale * cubic_coef * square)
    )
    return gelu_value, gelu_slope


class Spot:
    def __init__(self):
        me = lax.axis_index("fsdp")
        self.z = lax.axis_index("dp")
        self.c = lax.rem(me, 2)
        self.y = lax.rem(me // 2, RING)
        self.x = me // (2 * RING)

    def owner(self, i, j, c=None):
        c = self.c if c is None else c
        x = lax.rem(self.x + i * (1 - c) + j * c, RING)
        y = lax.rem(self.y + i * c + j * (1 - c), RING)
        return (x * RING + y) * 2 + c

    def sibling(self):
        return (self.x * RING + self.y) * 2 + (1 - self.c)


def greet(targets, meanwhile=None):
    barrier = pltpu.get_barrier_semaphore()
    for target in targets:
        pl.semaphore_signal(barrier, inc=1, device_id=target, device_id_type=MESH_ID)
    if meanwhile is not None:
        meanwhile()
    pl.semaphore_wait(barrier, len(targets))


class Mail:
    def __init__(self, send_sem, recv_sem):
        self.send_sem, self.recv_sem = send_sem, recv_sem
        self.keys, self.sent = {}, 0

    def copy(self, src, dst, target, n, lane):
        return pltpu.make_async_remote_copy(
            src_ref=src,
            dst_ref=dst,
            send_sem=self.send_sem.at[lane],
            recv_sem=self.recv_sem.at[n],
            device_id=target,
            device_id_type=MESH_ID,
        )

    def slot(self, key):
        return key if isinstance(key, int) else self.keys.setdefault(key, 2 + len(self.keys))

    def send(self, src, dst, target, key, lane=0):
        self.copy(src, dst, target, self.slot(key), lane).start()
        self.sent += 1

    def wait(self, dst, key, target):
        self.copy(dst, dst, target, self.slot(key), 0).wait_recv()

    def send_at(self, src, dst, target, n, lane):
        self.copy(src, dst, target, n, lane).start()

    def wait_at(self, dst, target, n):
        self.copy(dst, dst, target, n, 0).wait_recv()

    def sent_all(self, like, target, lane):
        self.copy(like, like, target, 0, lane).wait_send()


VM_K1 = 8 << 20
RING_COPIES = 30
SLOT_TOTAL = 128
DEAD = SLOT_TOTAL
BY_COL, BY_ROW, LAST, LIVE = 0, 1, 2, 3


def slot_tables(rows_ref, cols_ref, counts, tab_ref):
    n = SLOT_TOTAL
    lane = lax.broadcasted_iota(jnp.int32, (n, n), 1)
    sub = lax.broadcasted_iota(jnp.int32, (n, n), 0)
    lane_owner = lax.broadcasted_iota(jnp.int32, (8, n), 1) // SLOTS
    held = jnp.zeros((8, n), jnp.int32)
    for o in range(n // SLOTS):
        held = jnp.where(lane_owner == o, counts[o], held)
    lane_f, sub_f = lane.astype(F32), sub.astype(F32)

    def spread(row):
        across = jnp.broadcast_to(row.astype(F32), (n, n))
        return across, across.T

    held_l, held_s = spread(held[0:1])
    slot_l = lax.rem(lane, SLOTS).astype(F32)
    slot_s = lax.rem(sub, SLOTS).astype(F32)
    live_l = jnp.where(slot_l < held_l, 1.0, 0.0)
    live_s = jnp.where(slot_s < held_s, 1.0, 0.0)

    def order(key_l, key_s):
        tie = jnp.where(key_l == key_s, jnp.where(lane < sub, live_l, 0.0), 0.0)
        rank = jnp.sum(jnp.where(key_l < key_s, live_l, tie), axis=1, keepdims=True)
        hit = jnp.where(rank == lane_f, live_s, 0.0)
        return jnp.sum(hit * sub_f, axis=0, keepdims=True)

    col_l, col_s = spread(cols_ref[...])
    row_l, row_s = spread(rows_ref[...])
    upto = jnp.sum(jnp.where(col_s <= col_l, live_s, 0.0), axis=0, keepdims=True)
    last = jnp.where(live_l[0:1] > 0.5, upto - 1.0, float(DEAD))
    number = jnp.sum(live_s, axis=0, keepdims=True)
    for at, row in (
        (BY_COL, order(col_l, col_s)), (BY_ROW, order(row_l, row_s)), (LAST, last), (LIVE, number)
    ):
        tab_ref[at:at + 1, :] = row.astype(jnp.int32)


def gather_kernel(
    rows_hbm, cols_hbm, counts_hbm, up_ref, dn_ref, x_hbm, dy_hbm,
    gu_ref, gd_ref, x_ref, dy_ref, tab_ref, rows_ref, cols_ref, counts,
    own_sem, send_sem, recv_sem,
):
    spot = Spot()
    mine = (up_ref, dn_ref)
    full = (gu_ref, gd_ref)
    first_p, first_m = {"fsdp": spot.owner(1, 0)}, {"fsdp": spot.owner(3, 0)}
    second_p, second_m = {"fsdp": spot.owner(0, 1)}, {"fsdp": spot.owner(0, 3)}
    other = {"fsdp": spot.sibling()}
    mail = Mail(send_sem, recv_sem)
    me = spot.owner(0, 0)

    def held(i, j, h):
        return mine[h] if (i, j) == (0, 0) else full[h].at[spot.owner(i, j)]

    def place(i, j, h):
        return full[h].at[spot.owner(i, j)]

    def arrive(i, j, h, key, source):
        mail.wait(place(i, j, h), key, source)

    def share(i, j, h):
        mail.send(held(i, j, h), place(i, j, h), other, h, lane=1)

    def second(i, h):
        mail.send(held(i, 0, h), place(i, 0, h), second_p, ("sec", i, 3, h))
        mail.send(held(i, 0, h), place(i, 0, h), second_m, ("sec", i, 1, h))

    keeps = [
        pltpu.make_async_copy(src, dst, own_sem.at[n])
        for n, (src, dst) in enumerate((
            (up_ref, gu_ref.at[me]), (dn_ref, gd_ref.at[me]),
            (x_ref, x_ref), (dy_ref, dy_ref),
            (rows_hbm, rows_ref), (cols_hbm, cols_ref), (counts_hbm, counts),
        ))
    ]
    blocks = x_ref.shape[0]

    def cut(b, carry):
        at = pl.ds(pl.multiple_of(b * EDGE, EDGE), EDGE)
        pltpu.make_async_copy(x_hbm.at[:, at], x_ref.at[b], own_sem.at[2]).start()
        pltpu.make_async_copy(dy_hbm.at[:, at], dy_ref.at[b], own_sem.at[3]).start()
        return carry

    def load():
        for n in (4, 5, 6, 0, 1):
            keeps[n].start()
        lax.fori_loop(0, blocks, cut, 0)

    greet([first_p, first_m, second_p, second_m, other], load)
    for h in (0, 1):
        mail.send(mine[h], place(0, 0, h), first_p, ("fst", 3, h))
        mail.send(mine[1 - h], place(0, 0, 1 - h), first_m, ("fst", 1, 1 - h))
    for h in (0, 1):
        second(0, h)
    for h in (0, 1):
        share(0, 0, h)
    for n in (4, 5, 6):
        keeps[n].wait()
    slot_tables(rows_ref, cols_ref, counts, tab_ref)
    arrive(3, 0, 0, ("fst", 3, 0), first_m)
    mail.send(held(3, 0, 0), place(3, 0, 0), first_p, ("fst", 2, 0))
    arrive(1, 0, 1, ("fst", 1, 1), first_p)
    mail.send(held(1, 0, 1), place(1, 0, 1), first_m, ("fst", 2, 1))
    second(3, 0)
    second(1, 1)
    share(3, 0, 0)
    share(1, 0, 1)
    arrive(3, 0, 1, ("fst", 3, 1), first_m)
    second(3, 1)
    share(3, 0, 1)
    arrive(1, 0, 0, ("fst", 1, 0), first_p)
    second(1, 0)
    share(1, 0, 0)
    arrive(2, 0, 0, ("fst", 2, 0), first_m)
    second(2, 0)
    share(2, 0, 0)
    arrive(2, 0, 1, ("fst", 2, 1), first_p)
    second(2, 1)
    share(2, 0, 1)
    for i in (0, 3, 1, 2):
        arrive(i, 3, 0, ("sec", i, 3, 0), second_m)
        mail.send(held(i, 3, 0), place(i, 3, 0), second_p, ("sec", i, 2, 0))
        share(i, 3, 0)
        arrive(i, 1, 1, ("sec", i, 1, 1), second_p)
        mail.send(held(i, 1, 1), place(i, 1, 1), second_m, ("sec", i, 2, 1))
        share(i, 1, 1)
        arrive(i, 3, 1, ("sec", i, 3, 1), second_m)
        share(i, 3, 1)
        arrive(i, 1, 0, ("sec", i, 1, 0), second_p)
        share(i, 1, 0)
    for i in (0, 3, 1, 2):
        arrive(i, 2, 0, ("sec", i, 2, 0), second_m)
        share(i, 2, 0)
        arrive(i, 2, 1, ("sec", i, 2, 1), second_p)
        share(i, 2, 1)
    for h in (0, 1):
        mail.wait(full[h].at[pl.ds(0, RING * RING)], h, other)
    for n in range(4):
        keeps[n].wait()
    mail.sent_all(gu_ref.at[pl.ds(0, RING_COPIES)], other, 0)
    mail.sent_all(gu_ref, other, 1)
    assert len(mail.keys) == RING_COPIES and mail.sent == RING_COPIES + gu_ref.shape[0]


def gather_weights(rows, cols, counts, up, dn, x, dy):
    owners = 2 * RING * RING
    any_spec = pl.BlockSpec(memory_space=pltpu.HBM)
    vmem_spec = pl.BlockSpec(memory_space=pltpu.VMEM)
    full = pltpu.VMEM((owners,) + up.shape, up.dtype)
    cut = pltpu.VMEM((x.shape[1] // EDGE, x.shape[0], EDGE), x.dtype)
    return pl.pallas_call(
        gather_kernel,
        out_shape=(
            full, full, cut, cut,
            jax.ShapeDtypeStruct((8, SLOT_TOTAL), jnp.int32),
        ),
        in_specs=[any_spec] * 7,
        out_specs=(vmem_spec,) * 5,
        scratch_shapes=[
            pltpu.VMEM((1, SLOT_TOTAL), jnp.int32),
            pltpu.VMEM((1, SLOT_TOTAL), jnp.int32),
            pltpu.SMEM(counts.shape, jnp.int32),
            pltpu.SemaphoreType.DMA((7,)),
            pltpu.SemaphoreType.DMA((2,)),
            pltpu.SemaphoreType.DMA((2 + RING_COPIES,)),
        ],
        compiler_params=pltpu.CompilerParams(
            collective_id=0, has_side_effects=True, vmem_limit_bytes=VM_K1
        ),
        name="gather_weights",
    )(
        in_hbm(rows.reshape(1, SLOT_TOTAL)), in_hbm(cols.reshape(1, SLOT_TOTAL)), in_hbm(counts),
        in_hbm(up), in_hbm(dn), in_hbm(x), in_hbm(dy),
    )


NT = (((1,), (1,)), ((), ()))
TN = (((0,), (0,)), ((), ()))
NN = (((1,), (0,)), ((), ()))


def mm(a, b, dims):
    return lax.dot_general(a, b, dims, preferred_element_type=F32)


UNROLL, REST = 10, 2


def layer_kernel(
    rows, cols, tab, x, dy, up, dn, out_hbm, in_hbm, hid, pgr, out, inp, acc, sem
):
    row_blocks, tok = x.shape[:2]
    width = row_blocks * EDGE
    n_live = tab[LIVE, 0]
    whole = n_live // UNROLL
    rest = (n_live - whole * UNROLL + REST - 1) // REST

    def block(b):
        return pl.ds(pl.multiple_of(b * EDGE, EDGE), EDGE)

    hid[DEAD] = jnp.zeros((tok, EDGE), BF16)
    pgr[DEAD] = jnp.zeros((tok, EDGE), BF16)

    def forward(width, start, step, carry):
        pre, back = acc[0], acc[1]
        for u in range(width):
            s = start + step * width + u
            k = tab[BY_COL, jnp.minimum(s, n_live - 1)]
            before = tab[BY_COL, jnp.clip(s - 1, 0, n_live - 1)]
            r = rows[k]
            first = jnp.logical_or(s == 0, cols[before] != cols[k])
            pre = jnp.where(first, 0.0, pre) + mm(x[r], up[k], NN)
            back = jnp.where(first, 0.0, back) + mm(dy[r], dn[k], NT)
            value, slope = gelu_parts(pre)
            to = jnp.where(s < n_live, s, DEAD + 1)
            hid[to] = value.astype(BF16)
            pgr[to] = (back * slope).astype(BF16)
        acc[0] = pre
        acc[1] = back
        return carry

    lax.fori_loop(0, whole, functools.partial(forward, UNROLL, 0), 0)
    lax.fori_loop(0, rest, functools.partial(forward, REST, whole * UNROLL), 0)

    def clear(b, carry):
        out[:, block(b)] = jnp.zeros((tok, EDGE), BF16)
        inp[:, block(b)] = jnp.zeros((tok, EDGE), BF16)
        return carry

    lax.fori_loop(0, row_blocks, clear, 0)

    def put(b, carry):
        pltpu.make_async_copy(out.at[:, block(b)], out_hbm.at[:, block(b)], sem.at[0]).start()
        pltpu.make_async_copy(inp.at[:, block(b)], in_hbm.at[:, block(b)], sem.at[1]).start()
        return carry

    def backward(width, start, step, done):
        o, g = acc[0], acc[1]
        for u in range(width):
            t = start + step * width + u
            k = tab[BY_ROW, jnp.minimum(t, n_live - 1)]
            r = rows[k]
            before = tab[BY_ROW, jnp.clip(t - 1, 0, n_live - 1)]
            to = block(jnp.where(t < n_live, r, row_blocks))
            first = jnp.logical_or(t == 0, rows[before] != r)
            last = tab[LAST, k]
            o = jnp.where(first, 0.0, o) + mm(hid[last], dn[k], NN)
            g = jnp.where(first, 0.0, g) + mm(pgr[last], up[k], NT)
            out[:, to] = o.astype(BF16)
            inp[:, to] = g.astype(BF16)
        acc[0] = o
        acc[1] = g
        upto = rows[tab[BY_ROW, jnp.minimum(start + (step + 1) * width - 1, n_live - 1)]]
        lax.fori_loop(done, upto, put, 0)
        return upto

    done = lax.fori_loop(0, whole, functools.partial(backward, UNROLL, 0), 0)
    done = lax.fori_loop(0, rest, functools.partial(backward, REST, whole * UNROLL), done)
    lax.fori_loop(done, row_blocks, put, 0)
    every = pl.ds(0, width)
    pltpu.make_async_copy(out.at[:, every], out_hbm, sem.at[0]).wait()
    pltpu.make_async_copy(inp.at[:, every], in_hbm, sem.at[1]).wait()


def local_layer(rows, cols, tab, x, dy, up, dn):
    row_blocks, tok = x.shape[:2]
    width = row_blocks * EDGE
    any_spec = pl.BlockSpec(memory_space=pl.ANY)
    smem_spec = pl.BlockSpec(memory_space=pltpu.SMEM)
    vmem_spec = pl.BlockSpec(memory_space=pltpu.VMEM)
    kept = pltpu.VMEM((SLOT_TOTAL + 2, tok, EDGE), BF16)
    result = jax.ShapeDtypeStruct((tok, width), BF16)
    return pl.pallas_call(
        layer_kernel,
        out_shape=(result, result, kept, kept),
        in_specs=[smem_spec] * 3 + [vmem_spec] * 4,
        out_specs=(any_spec,) * 2 + (vmem_spec,) * 2,
        scratch_shapes=[
            pltpu.VMEM((tok, width + EDGE), BF16),
            pltpu.VMEM((tok, width + EDGE), BF16),
            pltpu.VMEM((2, tok, EDGE), F32),
            pltpu.SemaphoreType.DMA((2,)),
        ],
        compiler_params=pltpu.CompilerParams(vmem_limit_bytes=VM_K2),
        name="local_layer",
    )(
        rows, cols, tab, in_vmem(x), in_vmem(dy),
        in_vmem(up.reshape(SLOT_TOTAL, EDGE, EDGE)), in_vmem(dn.reshape(SLOT_TOTAL, EDGE, EDGE)),
    )


VM_K2 = 16 << 20


def in_hbm(array):
    return pltpu.with_memory_space_constraint(array, pltpu.HBM)


def in_vmem(array):
    return pltpu.with_memory_space_constraint(array, pltpu.VMEM)


TAIL = 4
RS_COPIES = 40 + 10 * TAIL
VM_K3 = 26 << 20


def scatter_kernel(
    scale, rows, tab, x, dy, hid, pgr, ug_ref, dg_ref,
    stage, own, sib, mid, got_m, got_p, r_own, r_bf, r_f32, mid2, fin_m, fin_p, zsend, zrecv,
    send_sem, recv_sem,
):
    spot = Spot()
    final = (ug_ref, dg_ref)
    first_p, first_m = {"fsdp": spot.owner(1, 0)}, {"fsdp": spot.owner(3, 0)}
    second_p, second_m = {"fsdp": spot.owner(0, 1)}, {"fsdp": spot.owner(0, 3)}
    other = {"fsdp": spot.sibling()}
    z_a = {"dp": spot.z + 1 - 2 * lax.rem(spot.z, 2)}
    z_b = {"dp": RING - 1 - spot.z}
    mail = Mail(send_sem, recv_sem)

    def partial(owner, h, q):
        k = owner * SLOTS + q
        if h == 0:
            return mm(x[rows[k]], pgr[tab[LAST, k]], TN)
        return mm(hid[tab[LAST, k]], dy[rows[k]], TN)

    def make(i, j):
        at = i * RING + j
        for h in (0, 1):
            for q in range(SLOTS):
                stage[at, h, q] = partial(spot.owner(i, j, 1 - spot.c), h, q).astype(BF16)

    def give(i, j):
        at = i * RING + j
        mail.send_at(stage.at[at], sib.at[at], other, at, 0)

    def given(i, j):
        at = i * RING + j
        mail.wait_at(sib.at[at], other, at)

    def keep(i, j, h, *more):
        at = i * RING + j
        for q in range(SLOTS):
            value = partial(spot.owner(i, j), h, q) + sib[at, h, q].astype(F32)
            for ref in more:
                value = value + ref[q].astype(F32)
            own[at, h, q] = value.astype(BF16)
        return own.at[at, h]

    shares = [pl.ds(p * SLOTS // TAIL, SLOTS // TAIL) for p in range(TAIL)]
    mids = RING * RING
    base = mids + 2 * RING
    one = base + 4 * RING

    def turns(*acts):
        def step(n, carry):
            for act in acts:
                act(turn(n))
            return carry
        return step

    def make_give(j):
        def act(i):
            make(i, j)
            give(i, j)
        return act

    def far(i):
        given(i, 2)
        mail.send_at(keep(i, 2, 0), mid.at[i, 0], second_p, mids + i, 1)
        mail.send_at(keep(i, 2, 1), mid.at[i, 1], second_m, mids + RING + i, 1)

    def near(i):
        given(i, 1)
        mail.send_at(keep(i, 1, 1), got_m.at[i, 1], second_p, base + i, 1)
        given(i, 3)
        mail.send_at(keep(i, 3, 0), got_p.at[i, 0], second_m, base + RING + i, 1)
        mail.wait_at(mid.at[i, 0], second_m, mids + i)
        mail.send_at(keep(i, 1, 0, mid.at[i, 0]), got_m.at[i, 0], second_p, base + 2 * RING + i, 1)
        mail.wait_at(mid.at[i, 1], second_p, mids + RING + i)
        mail.send_at(keep(i, 3, 1, mid.at[i, 1]), got_p.at[i, 1], second_m, base + 3 * RING + i, 1)

    def stay(i):
        given(i, 0)
        at = i * RING
        for h in (0, 1):
            for q in range(SLOTS):
                r_own[i, h, q] = partial(spot.owner(i, 0), h, q) + sib[at, h, q].astype(F32)

    def rung(i, h):
        mail.wait_at(got_m.at[i, h], second_m, base + (2 * RING, 0)[h] + i)
        mail.wait_at(got_p.at[i, h], second_p, base + (RING, 3 * RING)[h] + i)

    def ring_sum(i, h, of):
        return r_own[i, h, of] + got_m[i, h, of].astype(F32) + got_p[i, h, of].astype(F32)

    def pass_on(n, i, h, dst, target):
        rung(i, h)
        for p, of in enumerate(shares):
            r_bf[n, of] = ring_sum(i, h, of).astype(BF16)
            mail.send_at(r_bf.at[n, of], dst.at[h, of], target, one + 6 * p + n, 2)

    def add_on(p, of, n, i, h, dst, target):
        value = ring_sum(i, h, of)
        mail.wait_at(mid2.at[h, of], (first_m, first_p)[h], one + 6 * p + h)
        r_bf[4 + n, of] = (value + mid2[h, of].astype(F32)).astype(BF16)
        mail.send_at(r_bf.at[4 + n, of], dst.at[h, of], target, one + 6 * p + 4 + n, 2)

    greet(
        [first_p, first_m, second_p, second_m, other, z_a, z_b],
        lambda: lax.fori_loop(0, RING, turns(lambda i: make(i, 2)), 0),
    )
    lax.fori_loop(0, 4, turns(lambda i: give(i, 2)), 0)
    lax.fori_loop(0, 4, turns(far, make_give(3), make_give(1)), 0)
    lax.fori_loop(0, 4, turns(near), 0)
    lax.fori_loop(0, 4, turns(make_give(0)), 0)
    lax.fori_loop(0, 4, turns(stay), 0)
    pass_on(0, 2, 0, mid2, first_p)
    pass_on(1, 2, 1, mid2, first_m)
    pass_on(2, 1, 1, fin_m, first_p)
    pass_on(3, 3, 0, fin_p, first_m)
    rung(1, 0)
    rung(3, 1)
    for p, of in enumerate(shares):
        add_on(p, of, 0, 1, 0, fin_m, first_p)
        add_on(p, of, 1, 3, 1, fin_p, first_m)
    for h in (0, 1):
        rung(0, h)
        r_f32[h] = ring_sum(0, h, slice(None))
    plane = one + 6 * TAIL
    for p, of in enumerate(shares):
        for h in (0, 1):
            mail.wait_at(fin_m.at[h, of], first_m, one + 6 * p + (4, 2)[h])
            mail.wait_at(fin_p.at[h, of], first_p, one + 6 * p + (3, 5)[h])
            value = r_f32[h, of] + fin_m[h, of].astype(F32) + fin_p[h, of].astype(F32)
            zsend[0, h, of] = value.astype(BF16)
            mail.send_at(
                zsend.at[0, h, of], zrecv.at[0, h, of], (z_a, z_b)[h], plane + 4 * p + h, 2
            )
    for p, of in enumerate(shares):
        for h in (0, 1):
            mail.wait_at(zrecv.at[0, h, of], (z_a, z_b)[h], plane + 4 * p + h)
            value = zsend[0, h, of].astype(F32) + zrecv[0, h, of].astype(F32)
            zsend[1, h, of] = value.astype(BF16)
            mail.send_at(
                zsend.at[1, h, of], zrecv.at[1, h, of], (z_b, z_a)[h], plane + 4 * p + 2 + h, 2
            )
    for p, of in enumerate(shares):
        for h in (0, 1):
            mail.wait_at(zrecv.at[1, h, of], (z_b, z_a)[h], plane + 4 * p + 2 + h)
            value = zsend[1, h, of].astype(F32) + zrecv[1, h, of].astype(F32)
            final[h][of] = value * scale

    mail.sent_all(stage, other, 0)
    mail.sent_all(own.at[pl.ds(0, 3 * RING)], other, 1)
    mail.sent_all(own.at[pl.ds(0, 5)], other, 2)


def turn(n):
    return lax.rem(2 + n * (n + 1) // 2, RING)


def scatter_grads(rows, tab, x, dy, hid, pgr, scale):
    piece = (SLOTS, EDGE, EDGE)
    grad = jax.ShapeDtypeStruct(piece, F32)
    vmem = pl.BlockSpec(memory_space=pltpu.VMEM)
    smem = pl.BlockSpec(memory_space=pltpu.SMEM)
    return pl.pallas_call(
        functools.partial(scatter_kernel, scale),
        out_shape=(grad, grad),
        in_specs=[smem] * 2 + [vmem] * 4,
        out_specs=(vmem, vmem),
        scratch_shapes=[
            pltpu.VMEM((RING * RING, 2) + piece, BF16),
            pltpu.VMEM((RING * RING, 2) + piece, BF16),
            pltpu.VMEM((RING * RING, 2) + piece, BF16),
            pltpu.VMEM((RING, 2) + piece, BF16),
            pltpu.VMEM((RING, 2) + piece, BF16),
            pltpu.VMEM((RING, 2) + piece, BF16),
            pltpu.VMEM((RING, 2) + piece, F32),
            pltpu.VMEM((6,) + piece, BF16),
            pltpu.VMEM((2,) + piece, F32),
            pltpu.VMEM((2,) + piece, BF16),
            pltpu.VMEM((2,) + piece, BF16),
            pltpu.VMEM((2,) + piece, BF16),
            pltpu.VMEM((2, 2) + piece, BF16),
            pltpu.VMEM((2, 2) + piece, BF16),
            pltpu.SemaphoreType.DMA((3,)),
            pltpu.SemaphoreType.DMA((RS_COPIES,)),
        ],
        compiler_params=pltpu.CompilerParams(
            collective_id=1, has_side_effects=True, vmem_limit_bytes=VM_K3
        ),
        name="scatter_grads",
    )(rows, tab, in_vmem(x), in_vmem(dy), in_vmem(hid), in_vmem(pgr))


def on_device(tokens, cotangent, up_w, dn_w, block_rows, block_cols, owner_counts):
    devices = lax.axis_size("dp") * lax.axis_size("fsdp")
    scale = 1.0 / math.sqrt(tokens.shape[0] * devices)
    up_full, dn_full, x, dy, tab = gather_weights(
        block_rows, block_cols, owner_counts, up_w, dn_w, tokens, cotangent
    )
    output, input_grad, hid, pgr = local_layer(
        block_rows, block_cols, tab, x, dy, up_full, dn_full
    )
    up_grad, down_grad = scatter_grads(block_rows, tab, x, dy, hid, pgr, scale)
    return output, input_grad, up_grad, down_grad


def solution(mesh):
    in_specs = (
        P(("dp", "fsdp"), None),
        P(("dp", "fsdp"), None),
        P("fsdp", None, None),
        P("fsdp", None, None),
        P(),
        P(),
        P(),
    )
    out_specs = (
        P(("dp", "fsdp"), None),
        P(("dp", "fsdp"), None),
        P("fsdp", None, None),
        P("fsdp", None, None),
    )
    return jax.shard_map(
        on_device, mesh=mesh, in_specs=in_specs, out_specs=out_specs, check_vma=False
    )
```
